32 devices in a mesh: prow: 2 (over y), pcol: 16 (over z, x, core).
Axes of the slice: x: 2, y: 2, z: 4, core: 2. Of those that a mesh axis runs over, the one named last changes fastest.
Arguments:
- matrix: float32 [32, 2, 256, 4, 16, 256], P(None, 'prow', None, None, 'pcol'), may hold values from -6 to 6
- inverses: float32 [3, 256, 256], replicated, as said below
Outputs:
- factored: float32 [32, 2, 256, 4, 16, 256], P(None, 'prow', None, None, 'pcol')
The draws below stay inside these ranges and needn't reach their ends.
Inputs may be any that keep to these rules, and one draw needn't show every extreme that they name: Each of the 3 matrices of inverses is lower triangular with a positive diagonal.
All inputs are finite; a program needn't handle non-finite values.
Results may differ from the reference program's by a relative error of at most 0.0003.
Values sent between devices are 32-bit elements; how exact they have to be, the bound alone decides.
A program may use at most 256 MiB of HBM per device.

```python
import math
import jax
import jax.numpy as jnp
from jax import lax

N = 16384
NB = 256
STEPS = 3
RB = 32
CB = 4
N_PROW = 2
N_PCOL = 16


def draw_inverses(key, part):
    key_diag = jax.random.fold_in(key, 11)
    key_lower = jax.random.fold_in(key, 23)
    spread = 0.1 / math.sqrt(NB)
    diagonal = jax.random.uniform(key_diag, (STEPS, NB), jnp.float32, 0.13, 0.19)
    lower_part = jax.random.normal(key_lower, (STEPS, NB, NB), jnp.float32) * spread
    row_ids = jnp.arange(NB)[:, None]
    col_ids = jnp.arange(NB)[None, :]
    strict = jnp.where((row_ids > col_ids)[None], lower_part, 0.0)
    return strict + jnp.eye(NB, dtype=jnp.float32)[None] * diagonal[:, :, None]


def shard_levels(key, extent, pieces, least, top_value):
    def one(axis_at, parts):
        heights = jax.random.uniform(jax.random.fold_in(jax.random.fold_in(key, 6), axis_at), (parts,), jnp.float32, least / len(pieces), top_value / len(pieces))
        return jnp.repeat(jnp.exp(heights), extent[axis_at] // parts).reshape((-1,) + (1,) * (len(extent) - axis_at - 1))

    loudness = one(*pieces[0])
    for cut in pieces[1:]:
        loudness = loudness * one(*cut)
    return loudness


def bell_draw(key, dims, scale, most, split=(), held_as=jnp.bfloat16):
    drawn = jax.random.normal(key, dims, jnp.float32) * scale
    if len(split) > 0:
        drawn = shard_levels(key, dims, split, -0.22, 0.18) * drawn
    return jnp.clip(drawn, min=-most, max=most).astype(held_as)


def setup_inputs(seed: int = 0) -> dict:
    arg_keys = jax.random.split(jax.random.key(seed), 3)
    return {
        "matrix": bell_draw(arg_keys[0], (RB, N_PROW, NB, CB, N_PCOL, NB), 1.0, 6.0, ((1, 2), (4, 16)), jnp.float32),
        "inverses": draw_inverses(jax.random.fold_in(arg_keys[2], 71), 0),
    }


exact_precision = lax.Precision.HIGHEST


def reference(matrix, inverses):
    blocks_total = N // NB
    by_columns = matrix.transpose(3, 4, 0, 1, 2, 5).reshape(blocks_total, N, NB)
    row_index = jnp.arange(N, dtype=jnp.int32)
    for factor_step in range(STEPS):
        lower_edge = factor_step * NB
        upper_edge = lower_edge + NB
        column = by_columns[factor_step]
        panel = jnp.dot(column, inverses[factor_step].T, precision=exact_precision, preferred_element_type=jnp.float32)
        panel = jnp.where((row_index >= lower_edge)[:, None], panel, jnp.float32(0.0))

        def update_block(pair):
            block_values, block_index = pair
            partner = lax.dynamic_slice_in_dim(panel, (block_index * NB).astype(jnp.int32), NB, 0)
            product = jnp.dot(panel, partner.T, precision=exact_precision, preferred_element_type=jnp.float32)
            live_mask = (row_index >= upper_edge)[:, None] & (block_index > factor_step)
            return jnp.where(live_mask, block_values - product, block_values)

        by_columns = lax.map(update_block, (by_columns, jnp.arange(blocks_total, dtype=jnp.int32)))
        by_columns = by_columns.at[factor_step].set(panel)
    block_ids = jnp.arange(blocks_total, dtype=jnp.int32)
    col_index = block_ids[:, None] * NB + jnp.arange(NB, dtype=jnp.int32)[None, :]
    kept_mask = (row_index[None, :, None] >= col_index[:, None, :]) | (block_ids < STEPS)[:, None, None]
    by_columns = jnp.where(kept_mask, by_columns, jnp.float32(0.0))
    return by_columns.reshape(CB, N_PCOL, RB, N_PROW, NB, NB).transpose(2, 3, 4, 0, 1, 5)
```

```python
import functools

import jax
import jax.numpy as jnp
from jax import lax
from jax.experimental import pallas as pl
from jax.experimental.pallas import tpu as pltpu
from jax.sharding import PartitionSpec as P

STEPS = 3
SUB = 2
WINDOW = 8
LAG = 6
BACK = 8
MESH = pl.DeviceIdType.MESH
BF = jnp.bfloat16
F32 = jnp.float32


def split(value):
    high = value.astype(BF)
    return high, (value - high.astype(F32)).astype(BF)


def left(value):
    high, low = split(value)
    return jnp.concatenate([high, high, low], axis=1)


def right(value):
    high, low = split(value)
    return jnp.concatenate([high, low, high], axis=0)


def dot(a, b):
    return lax.dot_general(a, b, (((1,), (0,)), ((), ())), preferred_element_type=F32)


def kernel(
    n_prow, n_pcol, rb, cb, nb,
    a_hbm, inv_ref, out_hbm,
    panels, xch, sbuf, abuf, obuf, cst, ccol, prow_l,
    rsem, ssem, xrsem, xssem, asem, osem, srcsem,
):
    p = lax.axis_index("prow")
    q = lax.axis_index("pcol")
    depth = n_pcol // 4
    z, x, c = q // 4, (q // 2) % 2, q % 2
    sib = q + 1 - 2 * c
    xn = q + 2 - 4 * x
    sub = nb // SUB
    quarter = sub // 4
    chunks = rb * SUB
    lines = nb * cb * 2
    sub_lines = sub * cb * 2
    stride = cb * 2
    slots = 2 + cb
    top = (STEPS - 1) // n_prow + 1

    barrier = pltpu.get_barrier_semaphore()

    def greet(pp, qq):
        pl.semaphore_signal(barrier, inc=1, device_id=(pp, qq), device_id_type=MESH)

    greet(p, sib)
    greet(p, xn)
    pl.when(z > 0)(lambda: greet(p, q - 4))
    pl.when(z < depth - 1)(lambda: greet(p, q + 4))
    for d in range(1, n_prow):
        greet((p + d) % n_prow, q)
    peers = 1 + n_prow + (z > 0).astype(jnp.int32) + (z < depth - 1).astype(jnp.int32)

    def have(s, zz):
        a = s // SUB
        return (a < top) | (a * n_prow + p >= 4 * zz) | (zz <= 1)

    def rows(s, first, count):
        return pl.ds(pl.multiple_of(s * sub + first, quarter), count)

    def remote(ref, s, dev, si, ri):
        return pltpu.make_async_remote_copy(
            src_ref=ref, dst_ref=ref, send_sem=ssem.at[s % WINDOW, si], recv_sem=rsem.at[s, ri],
            device_id=(p, dev), device_id_type=MESH,
        )

    def cp_q(s, j, dev, si, ri):
        return remote(panels.at[:, rows(s, j * quarter, quarter), :], s, dev, si, ri)

    def cp_k(s, k, dev, si):
        return remote(panels.at[k, rows(s, 0, sub), :], s, dev, si, k)

    def cp_half(s, k, dev, si):
        return remote(panels.at[k, rows(s, sub // 2, sub // 2), :], s, dev, si, k)

    def cp_dn(s, j, dev, si, ri):
        return remote(panels.at[pl.ds(0, 2), rows(s, j * quarter, quarter), :], s, dev, si, ri)

    mine = 2 * x + c
    other = 2 * (1 - x) + c
    up = jnp.minimum(q + 4, n_pcol - 1)
    send_z = lambda s: cp_q(s, mine, up, 0, 0)
    send_x = lambda s: cp_q(s, mine, xn, 1, 1)
    send_c1 = lambda s: cp_q(s, mine, sib, 2, 2)
    send_c2 = lambda s: cp_q(s, other, sib, 3, 3)
    recv_z = lambda s: cp_q(s, mine, sib, 0, 0)
    recv_x = lambda s: cp_q(s, other, sib, 1, 1)
    recv_c1 = lambda s: cp_q(s, 2 * x + 1 - c, sib, 2, 2)
    recv_c2 = lambda s: cp_q(s, 2 * (1 - x) + 1 - c, sib, 3, 3)

    low = (z == 0) & (x == 1)
    above = (z == 1) & (x == 1)
    send_dn = lambda s: cp_dn(s, c, jnp.maximum(q - 4, 0), 4, 3)
    recv_dn = lambda s: cp_dn(s, c, sib, 4, 3)
    send_dc = lambda s: cp_dn(s, c, sib, 7, 4)
    recv_dc = lambda s: cp_dn(s, 1 - c, sib, 7, 4)

    def to_x(k):
        return (lambda s: cp_half(s, k, xn, 1 + 2 * k)) if k < 2 else (lambda s: cp_k(s, k, xn, 1 + 2 * k))

    def to_sib(k):
        return lambda s: cp_k(s, k, sib, 2 + 2 * k)

    def fwd(k):
        return (lambda s: cp_half(s, k, sib, 1 + 2 * k)) if k < 2 else (lambda s: cp_k(s, k, sib, 1 + 2 * k))

    def fwd_of(k):
        return k + 2 - 4 * ((k // 2) % 2)

    def always(s):
        return s >= 0

    def here(s):
        return have(s, z)

    def above_us(s):
        return have(s, z + 1)

    def start(fn, s, needed=always):
        @pl.when((s >= WINDOW) & needed(s - WINDOW))
        def _():
            fn(s - WINDOW).wait_send()

        pl.when(needed(s))(lambda: fn(s).start())

    def drain(fn, needed=always):
        for s in range(max(chunks - WINDOW, 0), chunks):
            pl.when(needed(s))(lambda: fn(s).wait_send())

    def block_of(slot):
        return slot + 1 if slot < 2 else (slot - 2) * n_pcol + q

    def cp_x(slot, s, part, d):
        return pltpu.make_async_remote_copy(
            src_ref=panels.at[:, rows(s, 0, sub), :], dst_ref=xch.at[slot, :, pl.ds(part * sub, sub), :],
            send_sem=xssem.at[slot, part, d], recv_sem=xrsem.at[slot, part],
            device_id=((p + d) % n_prow, q), device_id_type=MESH,
        )

    def cp_l(slot, s, part):
        return pltpu.make_async_copy(
            panels.at[:, rows(s, 0, sub), :], xch.at[slot, :, pl.ds(part * sub, sub), :], xrsem.at[slot, part])

    def publish(s):
        for slot in range(slots):
            g = block_of(slot)
            for part in range(SUB):
                @pl.when((g % n_prow == p) & ((g // n_prow) * SUB + part == s))
                def _():
                    for d in range(1, n_prow):
                        cp_x(slot, s, part, d).start()
                    cp_l(slot, s, part).start()

    def wait_slot(slot):
        g = block_of(slot)

        @pl.when(g % n_prow == p)
        def _():
            for part in range(SUB):
                cp_l(slot, 0, part).wait()

        @pl.when(g % n_prow != p)
        def _():
            for part in range(SUB):
                cp_x(slot, 0, part, 1).wait_recv()

    def a_in(a):
        return pltpu.make_async_copy(
            a_hbm.at[pl.ds(pl.multiple_of(a * lines, lines), lines), :], abuf.at[a % 2], asem.at[a % 2])

    def o_out(a):
        return pltpu.make_async_copy(
            obuf.at[a % 2], out_hbm.at[pl.ds(pl.multiple_of(a * lines, lines), lines), :], osem.at[a % 2])

    def s_in(s):
        return pltpu.make_async_copy(
            a_hbm.at[pl.ds(pl.multiple_of(s * sub_lines, sub_lines), sub_lines), :], sbuf.at[s % 2], srcsem.at[s % 2])

    @pl.when(q < STEPS)
    def _():
        s_in(0).start()

    a_in(0).start()
    pl.semaphore_wait(barrier, peers)

    def factor(k, m):
        return cst[k, m * 3 * nb:(m + 1) * 3 * nb, :]

    def factors():
        def mul(u, v):
            return dot(left(u), right(v))

        r00, r11, r22 = inv_ref[0].T, inv_ref[1].T, inv_ref[2].T
        w10 = mul(xch[0, 0], r00)
        w20 = mul(xch[1, 0], r00)
        r01 = -mul(mul(r00, w10.T), r11)
        w21 = mul(xch[1, 0], r01) + mul(xch[1, 1], r11)
        r02 = -mul(mul(r00, w20.T) + mul(r01, w21.T), r22)
        r12 = -mul(mul(r11, w21.T), r22)
        for k, column in enumerate(((r00,), (r01, r11), (r02, r12, r22))):
            for m, value in enumerate(column):
                cst[k, m * 3 * nb:(m + 1) * 3 * nb, :] = right(value)

    def columns(b, gb):
        @pl.when(gb >= STEPS)
        def _():
            raw = jnp.concatenate([left(xch[2 + b, m]) for m in range(STEPS)], axis=1)
            solved = [
                right(dot(raw[:, :(k + 1) * 3 * nb], cst[k, :(k + 1) * 3 * nb, :]).T) for k in range(STEPS)]
            for m in range(STEPS):
                total = jnp.zeros((nb, nb), F32)
                for k in range(m, STEPS):
                    f = factor(k, m)
                    total += dot(jnp.concatenate([f[:nb], f[:nb], f[nb:2 * nb]], axis=1), solved[k])
                ccol[b, m * 3 * nb:(m + 1) * 3 * nb, :] = right(total)

        if b == 0:
            for k in range(STEPS):
                @pl.when(gb == k)
                def _():
                    for m in range(STEPS):
                        ccol[b, m * 3 * nb:(m + 1) * 3 * nb, :] = (
                            -factor(k, m) if m <= k else jnp.zeros((3 * nb, nb), BF))

    def block(a, g, b):
        gb = block_of(2 + b)
        par = a % 2

        def put(value):
            for h in range(2):
                obuf[par, pl.ds(b * 2 + h, nb, stride=stride), :] = value[:, h * 128:(h + 1) * 128]

        def product():
            return dot(prow_l[...], ccol[b])

        def updated():
            old = jnp.concatenate(
                [abuf[par, pl.ds(b * 2 + h, nb, stride=stride), :] for h in range(2)], axis=1)
            return old - product()

        @pl.when((gb >= STEPS) & (g > gb))
        def _():
            put(updated())

        @pl.when((gb >= STEPS) & (g == gb))
        def _():
            down = lax.broadcasted_iota(jnp.int32, (nb, nb), 0)
            across = lax.broadcasted_iota(jnp.int32, (nb, nb), 1)
            put(jnp.where(down >= across, updated(), 0.0))

        @pl.when(g < gb)
        def _():
            put(jnp.zeros((nb, nb), F32))

        if b == 0:
            @pl.when((gb < STEPS) & (g >= gb))
            def _():
                put(-product())

    def compute(u):
        a = u // SUB
        g = a * n_prow + p

        @pl.when(u % SUB == 0)
        def _():
            @pl.when(a + 1 < rb)
            def _():
                a_in(a + 1).start()

            @pl.when(a == 0)
            def _():
                wait_slot(0)
                wait_slot(1)
                factors()

            for b in range(cb):
                gb = block_of(2 + b)

                @pl.when(a == jnp.minimum((gb - p + n_prow - 1) // n_prow, rb - 1))
                def _():
                    wait_slot(2 + b)
                    columns(b, gb)

            @pl.when(g >= q)
            def _():
                for k in range(STEPS):
                    prow_l[:, k * 3 * nb:(k + 1) * 3 * nb] = left(
                        panels[k, pl.ds(pl.multiple_of(a * nb, nb), nb), :])

            @pl.when(a >= 2)
            def _():
                o_out(a - 2).wait()
            a_in(a).wait()
            for b in range(cb // 2):
                block(a, g, b)

        @pl.when(u % SUB == SUB - 1)
        def _():
            for b in range(cb // 2, cb):
                block(a, g, b)
            o_out(a).start()

    def step(t, carry):
        @pl.when(t < chunks)
        def _():
            s = t

            @pl.when(z > 0)
            def _():
                pl.when(here(s))(lambda: recv_z(s).wait_recv())
                pl.when(z < depth - 1)(lambda: start(send_z, s, above_us))
                start(send_x, s, here)
                start(send_c1, s, here)

            for k in range(STEPS):
                @pl.when(q == k)
                def _():
                    s_in(s).wait()

                    @pl.when(s + 1 < chunks)
                    def _():
                        s_in(s + 1).start()
                    for h in range(2):
                        panels[k, rows(s, 0, sub), h * 128:(h + 1) * 128] = sbuf[s % 2, pl.ds(h, sub, stride=stride), :]
                    start(to_x(k), s)
                    start(to_sib(k), s)

        @pl.when((t >= 2) & (t < chunks + 2))
        def _():
            s = t - 2

            @pl.when(z > 0)
            def _():
                pl.when(here(s))(lambda: recv_x(s).wait_recv())
                start(send_c2, s, here)

            pl.when(above)(lambda: start(send_dn, s, here))

            for k in range(STEPS):
                @pl.when(q == fwd_of(k))
                def _():
                    fwd(k)(s).wait_recv()
                    start(fwd(k), s)

        @pl.when((t >= 3) & (t < chunks + 3))
        def _():
            s = t - 3

            @pl.when((z > 0) & here(s))
            def _():
                recv_c1(s).wait_recv()
                recv_c2(s).wait_recv()

            @pl.when(z == 0)
            def _():
                for k in range(STEPS):
                    same = k + 1 - 2 * (k % 2)

                    @pl.when(q == same)
                    def _():
                        cp_k(s, k, sib, 1 + 2 * k).wait_recv()

                    @pl.when((q != k) & (q != same) & (q != fwd_of(k)))
                    def _():
                        fwd(k)(s).wait_recv()
                start(send_z, s, above_us)

            pl.when(jnp.logical_not(low) & here(s))(lambda: publish(s))

        @pl.when(low & (t >= 3 + BACK) & (t < chunks + 3 + BACK))
        def _():
            s = t - 3 - BACK
            arrive_dn(s)

        @pl.when(low & (t >= 4 + BACK) & (t < chunks + 4 + BACK))
        def _():
            s = t - 4 - BACK
            recv_dc(s).wait_recv()
            publish(s)

        @pl.when((t >= lag) & (t < chunks + lag))
        def _():
            compute(t - lag)

        return carry

    def arrive_dn(s):
        recv_dn(s).wait_recv()
        start(send_dc, s)

    lag = jnp.where(low, 4 + BACK + LAG, 3 + LAG)
    lax.fori_loop(0, chunks + 4 + BACK + LAG, step, 0)

    pl.when(z < depth - 1)(lambda: drain(send_z, above_us))

    @pl.when(z > 0)
    def _():
        drain(send_x, here)
        drain(send_c1, here)
        drain(send_c2, here)

    pl.when(above)(lambda: drain(send_dn, here))
    pl.when(low)(lambda: drain(send_dc))

    for k in range(STEPS):
        @pl.when(q == k)
        def _():
            drain(to_x(k))
            drain(to_sib(k))

        @pl.when(q == fwd_of(k))
        def _():
            drain(fwd(k))
    for slot in range(slots):
        @pl.when(block_of(slot) % n_prow == p)
        def _():
            for part in range(SUB):
                for d in range(1, n_prow):
                    cp_x(slot, 0, part, d).wait_send()
    for a in range(max(rb - 2, 0), rb):
        o_out(a).wait()


def per_device(n_prow, n_pcol, matrix, inverses):
    rb, _, nb, cb, _, _ = matrix.shape
    lines = matrix.reshape(rb * nb * cb * 2, nb // 2)
    vmem = pltpu.VMEM
    dma = pltpu.SemaphoreType.DMA
    out = pl.pallas_call(
        functools.partial(kernel, n_prow, n_pcol, rb, cb, nb),
        out_shape=jax.ShapeDtypeStruct(lines.shape, F32),
        in_specs=[
            pl.BlockSpec(memory_space=pl.ANY),
            pl.BlockSpec(memory_space=pltpu.VMEM),
        ],
        out_specs=pl.BlockSpec(memory_space=pl.ANY),
        scratch_shapes=[
            vmem((STEPS, rb * nb, nb), F32),
            vmem((2 + cb, STEPS, nb, nb), F32),
            vmem((2, nb // SUB * cb * 2, 128), F32),
            vmem((2, nb * cb * 2, 128), F32),
            vmem((2, nb * cb * 2, 128), F32),
            vmem((STEPS, 3 * STEPS * nb, nb), BF),
            vmem((cb, 3 * STEPS * nb, nb), BF),
            vmem((nb, 3 * STEPS * nb), BF),
            dma((rb * SUB, 5)),
            dma((WINDOW, 8)),
            dma((2 + cb, SUB)),
            dma((2 + cb, SUB, n_prow)),
            dma((2,)),
            dma((2,)),
            dma((2,)),
        ],
        compiler_params=pltpu.CompilerParams(
            collective_id=0, has_side_effects=True, vmem_limit_bytes=58 * 1024 * 1024
        ),
    )(lines, inverses)
    return out.reshape(matrix.shape)


def solution(mesh):
    in_specs = (P(None, "prow", None, None, "pcol", None), P())
    out_specs = P(None, "prow", None, None, "pcol", None)
    return jax.shard_map(
        functools.partial(per_device, mesh.shape["prow"], mesh.shape["pcol"]),
        mesh=mesh, in_specs=in_specs, out_specs=out_specs, check_vma=False,
    )
```

```python
import functools

import jax
import jax.numpy as jnp
from jax import lax
from jax.experimental import pallas as pl
from jax.experimental.pallas import tpu as pltpu
from jax.sharding import PartitionSpec as P

STEPS = 3
SUB = 2
WINDOW = 8
LAG = 8
BACK = 8
DEEP = 4
MESH = pl.DeviceIdType.MESH
BF = jnp.bfloat16
F32 = jnp.float32


def split(value):
    high = value.astype(BF)
    return high, (value - high.astype(F32)).astype(BF)


def left(value):
    high, low = split(value)
    return jnp.concatenate([high, high, low], axis=1)


def right(value):
    high, low = split(value)
    return jnp.concatenate([high, low, high], axis=0)


def dot(a, b):
    return lax.dot_general(a, b, (((1,), (0,)), ((), ())), preferred_element_type=F32)


def gather(
    n_prow, n_pcol, rb, cb, nb,
    a_hbm, inv_ref, panels,
    xch, sbuf, cst,
    rsem, ssem, xrsem, xssem, srcsem,
):
    p = lax.axis_index("prow")
    q = lax.axis_index("pcol")
    depth = n_pcol // 4
    z, x, c = q // 4, (q // 2) % 2, q % 2
    sib = q + 1 - 2 * c
    xn = q + 2 - 4 * x
    sub = nb // SUB
    quarter = sub // 4
    chunks = rb * SUB
    sub_lines = sub * cb * 2
    stride = cb * 2
    slots = 2 + cb
    level = min(n_pcol // n_prow, rb)

    barrier = pltpu.get_barrier_semaphore()

    def greet(pp, qq):
        pl.semaphore_signal(barrier, inc=1, device_id=(pp, qq), device_id_type=MESH)

    greet(p, sib)
    greet(p, xn)
    pl.when(z > 0)(lambda: greet(p, q - 4))
    pl.when(z < depth - 1)(lambda: greet(p, q + 4))
    for d in range(1, n_prow):
        greet((p + d) % n_prow, q)
    peers = 1 + n_prow + (z > 0).astype(jnp.int32) + (z < depth - 1).astype(jnp.int32)

    def place(i):
        a = jnp.where(i < level, i, rb - 1 + level - i)
        if rb > level + 2:
            swapped = jnp.where(a == level + 1, level + 2, jnp.where(a == level + 2, level + 1, a))
            a = jnp.where(i < level, a, swapped)
        return a

    def chunk(n):
        return place(n // SUB) * SUB + n % SUB

    def block_row(n):
        return place(n // SUB) * n_prow + p

    def near(n):
        return block_row(n) < 4

    def far(n):
        return block_row(n) >= 4

    def have(n, zz):
        g = block_row(n)
        return (g == 1) | (g == 2) | (g >= 4 * zz)

    def rows(n, first, count):
        return pl.ds(pl.multiple_of(chunk(n) * sub + first, quarter), count)

    def remote(ref, n, dev, si, ri):
        return pltpu.make_async_remote_copy(
            src_ref=ref, dst_ref=ref, send_sem=ssem.at[n % WINDOW, si], recv_sem=rsem.at[n, ri],
            device_id=(p, dev), device_id_type=MESH,
        )

    def cp_q(n, count, j, dev, si, ri):
        return remote(panels.at[pl.ds(0, count), rows(n, j * quarter, quarter), :], n, dev, si, ri)

    def cp_k(n, k, dev, si):
        return remote(panels.at[k, rows(n, 0, sub), :], n, dev, si, k)

    def cp_half(n, k, dev, si):
        return remote(panels.at[k, rows(n, sub // 2, sub // 2), :], n, dev, si, k)

    def either(when, yes, no, needed):
        def act(method, n):
            pl.when(needed(n) & when(n))(lambda: getattr(yes(n), method)())
            pl.when(needed(n) & jnp.logical_not(when(n)))(lambda: getattr(no(n), method)())
        return act

    def only(copy, needed):
        return lambda method, n: pl.when(needed(n))(lambda: getattr(copy(n), method)())

    def start(act, n):
        pl.when(n >= WINDOW)(lambda: act("wait_send", n - WINDOW))
        act("start", n)

    def drain(act):
        for n in range(max(chunks - WINDOW, 0), chunks):
            act("wait_send", jnp.int32(n))

    def always(n):
        return n >= 0

    def here(n):
        return have(n, z)

    def beyond(n):
        return have(n, z + 1)

    mine = 2 * x + c
    other = 2 * (1 - x) + c
    up = jnp.minimum(q + 4, n_pcol - 1)

    def quarters(j, dev, si, needed):
        return either(near, lambda n: cp_q(n, 2, j, dev, si, si), lambda n: cp_q(n, STEPS, j, dev, si, si), needed)

    z_out = quarters(mine, up, 0, beyond)
    x_out = quarters(mine, xn, 1, here)
    c1_out = quarters(mine, sib, 2, here)
    c2_out = quarters(other, sib, 3, here)
    z_in = quarters(mine, sib, 0, here)
    x_in = quarters(other, sib, 1, here)
    c1_in = quarters(2 * x + 1 - c, sib, 2, here)
    c2_in = quarters(2 * (1 - x) + 1 - c, sib, 3, here)

    low = (z == 0) & (x == 1)
    above = (z == 1) & (x == 1)

    def two(j, dev, si, ri):
        return only(lambda n: cp_q(n, 2, j, dev, si, ri), far)

    dn_out = two(c, jnp.maximum(q - 4, 0), 4, 3)
    dn_in = two(c, sib, 4, 3)
    dc_out = two(c, sib, 7, 4)
    dc_in = two(1 - c, sib, 7, 4)

    def hop(k, dev):
        whole = lambda n: cp_k(n, k, dev, 1 + 2 * k)
        if k < 2:
            return either(near, whole, lambda n: cp_half(n, k, dev, 1 + 2 * k), always)
        return only(whole, always)

    def to_x(k):
        return hop(k, xn)

    def to_sib(k):
        return only(lambda n: cp_k(n, k, sib, 2 + 2 * k), always)

    def fwd(k):
        return hop(k, sib)

    def fwd_of(k):
        return k + 2 - 4 * ((k // 2) % 2)

    def block_of(slot):
        return slot + 1 if slot < 2 else (slot - 2) * n_pcol + q

    def depth_of(slot):
        return min(slot + 1, STEPS)

    def used(slot):
        return block_of(slot) >= (0 if slot < 2 else STEPS)

    def cp_x(slot, n, part, d):
        return pltpu.make_async_remote_copy(
            src_ref=panels.at[pl.ds(0, depth_of(slot)), rows(n, 0, sub), :],
            dst_ref=xch.at[slot, pl.ds(0, depth_of(slot)), pl.ds(part * sub, sub), :],
            send_sem=xssem.at[slot, part, d], recv_sem=xrsem.at[slot, part],
            device_id=((p + d) % n_prow, q), device_id_type=MESH,
        )

    def cp_l(slot, n, part):
        return pltpu.make_async_copy(
            panels.at[pl.ds(0, depth_of(slot)), rows(n, 0, sub), :],
            xch.at[slot, pl.ds(0, depth_of(slot)), pl.ds(part * sub, sub), :], xrsem.at[slot, part])

    def publish(n):
        for slot in range(slots):
            g = block_of(slot)
            for part in range(SUB):
                @pl.when(used(slot) & (g % n_prow == p) & ((g // n_prow) * SUB + part == chunk(n)))
                def _():
                    for d in range(1, n_prow):
                        cp_x(slot, n, part, d).start()
                    cp_l(slot, n, part).start()

    def wait_slot(slot):
        g = block_of(slot)

        @pl.when(used(slot) & (g % n_prow == p))
        def _():
            for part in range(SUB):
                cp_l(slot, 0, part).wait()

        @pl.when(used(slot) & (g % n_prow != p))
        def _():
            for part in range(SUB):
                cp_x(slot, 0, part, 1).wait_recv()

    def s_in(n):
        return pltpu.make_async_copy(
            a_hbm.at[pl.ds(pl.multiple_of(chunk(n) * sub_lines, sub_lines), sub_lines), :],
            sbuf.at[n % 2], srcsem.at[n % 2])

    @pl.when(q < STEPS)
    def _():
        s_in(jnp.int32(0)).start()

    pl.semaphore_wait(barrier, peers)

    def factor(k, m):
        return cst[k, m * 3 * nb:(m + 1) * 3 * nb, :]

    def factors():
        def mul(u, v):
            return dot(left(u), right(v))

        r00, r11, r22 = inv_ref[0].T, inv_ref[1].T, inv_ref[2].T
        w10 = mul(xch[0, 0], r00)
        w20 = mul(xch[1, 0], r00)
        r01 = -mul(mul(r00, w10.T), r11)
        w21 = mul(xch[1, 0], r01) + mul(xch[1, 1], r11)
        r02 = -mul(mul(r00, w20.T) + mul(r01, w21.T), r22)
        r12 = -mul(mul(r11, w21.T), r22)
        for k, column in enumerate(((r00,), (r01, r11), (r02, r12, r22))):
            for m, value in enumerate(column):
                cst[k, m * 3 * nb:(m + 1) * 3 * nb, :] = right(value)

    def columns(b, gb):
        @pl.when(gb >= STEPS)
        def _():
            raw = jnp.concatenate([left(xch[2 + b, m]) for m in range(STEPS)], axis=1)
            solved = [
                right(dot(raw[:, :(k + 1) * 3 * nb], cst[k, :(k + 1) * 3 * nb, :]).T) for k in range(STEPS)]
            for m in range(STEPS):
                total = jnp.zeros((nb, nb), F32)
                for k in range(m, STEPS):
                    f = factor(k, m)
                    total += dot(jnp.concatenate([f[:nb], f[:nb], f[nb:2 * nb]], axis=1), solved[k])
                panels[m, (rb + b) * nb:(rb + b + 1) * nb, :] = total

        if b == 0:
            for k in range(STEPS):
                @pl.when(gb == k)
                def _():
                    for m in range(STEPS):
                        if m <= k:
                            f = factor(k, m)
                            value = -(f[:nb].astype(F32) + f[nb:2 * nb].astype(F32))
                        else:
                            value = jnp.zeros((nb, nb), F32)
                        panels[m, (rb + b) * nb:(rb + b + 1) * nb, :] = value

    def ready(g):
        a = g // n_prow
        i = jnp.where(a < level, a, rb - 1 + level - a)
        if rb > level + 2:
            i = jnp.where(a == level + 1, rb - 3, jnp.where(a == level + 2, rb - 2, i))
        return i * SUB + SUB - 1

    def tables(t):
        first = max(g // n_prow for g in (1, 2)) * SUB + SUB - 1

        @pl.when(t == first)
        def _():
            wait_slot(0)
            wait_slot(1)
            factors()

        for b in range(cb):
            gb = block_of(2 + b)

            @pl.when(t == jnp.maximum(ready(gb), first))
            def _():
                wait_slot(2 + b)
                columns(b, gb)

    def step(t, carry):
        @pl.when(t < chunks)
        def _():
            n = t

            @pl.when(z > 0)
            def _():
                z_in("wait_recv", n)
                pl.when(z < depth - 1)(lambda: start(z_out, n))
                start(x_out, n)
                start(c1_out, n)

            for k in range(STEPS):
                @pl.when(q == k)
                def _():
                    s_in(n).wait()

                    @pl.when(n + 1 < chunks)
                    def _():
                        s_in(n + 1).start()
                    for h in range(2):
                        panels[k, rows(n, 0, sub), h * 128:(h + 1) * 128] = sbuf[n % 2, pl.ds(h, sub, stride=stride), :]
                    start(to_x(k), n)
                    start(to_sib(k), n)

        @pl.when((t >= 2) & (t < chunks + 2))
        def _():
            n = t - 2

            @pl.when(z > 0)
            def _():
                x_in("wait_recv", n)
                start(c2_out, n)

            pl.when(above)(lambda: start(dn_out, n))

            for k in range(STEPS):
                @pl.when(q == fwd_of(k))
                def _():
                    fwd(k)("wait_recv", n)
                    start(fwd(k), n)

        @pl.when((t >= 3) & (t < chunks + 3))
        def _():
            n = t - 3

            @pl.when(z > 0)
            def _():
                c1_in("wait_recv", n)
                c2_in("wait_recv", n)

            @pl.when(z == 0)
            def _():
                for k in range(STEPS):
                    same = k + 1 - 2 * (k % 2)

                    @pl.when(q == same)
                    def _():
                        to_sib(k)("wait_recv", n)

                    @pl.when((q != k) & (q != same) & (q != fwd_of(k)))
                    def _():
                        fwd(k)("wait_recv", n)
                start(z_out, n)

            pl.when(jnp.logical_not(low) & ((z == 0) | here(n)))(lambda: publish(n))

        @pl.when(low & (t >= 3 + BACK) & (t < chunks + 3 + BACK))
        def _():
            n = t - 3 - BACK
            dn_in("wait_recv", n)
            start(dc_out, n)

        @pl.when(low & (t >= 4 + BACK) & (t < chunks + 4 + BACK))
        def _():
            n = t - 4 - BACK
            dc_in("wait_recv", n)
            publish(n)

        tables(t - lag)
        return carry

    lag = jnp.where(low, 4 + BACK + LAG, 3 + LAG)
    lax.fori_loop(0, chunks + 4 + BACK + LAG, step, 0)

    pl.when(z < depth - 1)(lambda: drain(z_out))

    @pl.when(z > 0)
    def _():
        drain(x_out)
        drain(c1_out)
        drain(c2_out)

    pl.when(above)(lambda: drain(dn_out))
    pl.when(low)(lambda: drain(dc_out))

    for k in range(STEPS):
        @pl.when(q == k)
        def _():
            drain(to_x(k))
            drain(to_sib(k))

        @pl.when(q == fwd_of(k))
        def _():
            drain(fwd(k))
    for slot in range(slots):
        @pl.when(used(slot) & (block_of(slot) % n_prow == p))
        def _():
            for part in range(SUB):
                for d in range(1, n_prow):
                    cp_x(slot, 0, part, d).wait_send()


def update(n_prow, n_pcol, rb, cb, nb, a_hbm, panels, out_hbm, abuf, obuf, ccol, prow_l, asem, osem):
    p = lax.axis_index("prow")
    q = lax.axis_index("pcol")
    lines = nb * cb * 2
    stride = cb * 2
    group = rb // cb

    def place(i):
        return (i % cb) * group + i // cb

    def span(i):
        return pl.ds(pl.multiple_of(place(i) * lines, lines), lines)

    def live(i):
        return place(i) * n_prow + p >= q

    def a_in(i):
        return pltpu.make_async_copy(a_hbm.at[span(i), :], abuf.at[i % DEEP], asem.at[i % DEEP])

    def o_out(i):
        return pltpu.make_async_copy(obuf.at[i % DEEP], out_hbm.at[span(i), :], osem.at[i % DEEP])

    def block(i, g, b):
        gb = b * n_pcol + q
        par = i % DEEP

        def put(value):
            for h in range(2):
                obuf[par, pl.ds(b * 2 + h, nb, stride=stride), :] = value[:, h * 128:(h + 1) * 128]

        def product():
            return dot(prow_l[...], ccol[b])

        def updated():
            old = jnp.concatenate(
                [abuf[par, pl.ds(b * 2 + h, nb, stride=stride), :] for h in range(2)], axis=1)
            return old - product()

        @pl.when((gb >= STEPS) & (g > gb))
        def _():
            put(updated())

        @pl.when((gb >= STEPS) & (g == gb))
        def _():
            down = lax.broadcasted_iota(jnp.int32, (nb, nb), 0)
            across = lax.broadcasted_iota(jnp.int32, (nb, nb), 1)
            put(jnp.where(down >= across, updated(), 0.0))

        @pl.when(g < gb)
        def _():
            put(jnp.zeros((nb, nb), F32))

        if b == 0:
            @pl.when((gb < STEPS) & (g >= gb))
            def _():
                put(-product())

    for i in range(min(DEEP, rb)):
        pl.when(live(i))(lambda: a_in(i).start())
    for b in range(cb):
        for m in range(STEPS):
            ccol[b, m * 3 * nb:(m + 1) * 3 * nb, :] = right(panels[m, (rb + b) * nb:(rb + b + 1) * nb, :])

    def step(i, carry):
        a = place(i)
        g = a * n_prow + p

        @pl.when(i >= DEEP)
        def _():
            o_out(i - DEEP).wait()

        @pl.when(live(i))
        def _():
            a_in(i).wait()
            for k in range(STEPS):
                prow_l[:, k * 3 * nb:(k + 1) * 3 * nb] = left(panels[k, pl.ds(pl.multiple_of(a * nb, nb), nb), :])
        for b in range(cb):
            block(i, g, b)
        o_out(i).start()

        @pl.when((i + DEEP < rb) & live(i + DEEP))
        def _():
            a_in(i + DEEP).start()
        return carry

    lax.fori_loop(0, rb, step, 0)
    for i in range(max(rb - DEEP, 0), rb):
        o_out(i).wait()


def per_device(n_prow, n_pcol, matrix, inverses):
    rb, _, nb, cb, _, _ = matrix.shape
    lines = matrix.reshape(rb * nb * cb * 2, nb // 2)
    vmem = pltpu.VMEM
    dma = pltpu.SemaphoreType.DMA
    anywhere = pl.BlockSpec(memory_space=pl.ANY)
    inside = pl.BlockSpec(memory_space=pltpu.VMEM)
    panels = pl.pallas_call(
        functools.partial(gather, n_prow, n_pcol, rb, cb, nb),
        out_shape=vmem((STEPS, (rb + cb) * nb, nb), F32),
        in_specs=[anywhere, inside],
        out_specs=inside,
        scratch_shapes=[
            vmem((2 + cb, STEPS, nb, nb), F32),
            vmem((2, nb // SUB * cb * 2, 128), F32),
            vmem((STEPS, 3 * STEPS * nb, nb), BF),
            dma((rb * SUB, 5)),
            dma((WINDOW, 8)),
            dma((2 + cb, SUB)),
            dma((2 + cb, SUB, n_prow)),
            dma((2,)),
        ],
        compiler_params=pltpu.CompilerParams(
            collective_id=0, has_side_effects=True, vmem_limit_bytes=20 * 1024 * 1024
        ),
    )(lines, inverses)
    out = pl.pallas_call(
        functools.partial(update, n_prow, n_pcol, rb, cb, nb),
        out_shape=jax.ShapeDtypeStruct(lines.shape, F32),
        in_specs=[anywhere, inside],
        out_specs=anywhere,
        scratch_shapes=[
            vmem((DEEP, nb * cb * 2, 128), F32),
            vmem((DEEP, nb * cb * 2, 128), F32),
            vmem((cb, 3 * STEPS * nb, nb), BF),
            vmem((nb, 3 * STEPS * nb), BF),
            dma((DEEP,)),
            dma((DEEP,)),
        ],
        compiler_params=pltpu.CompilerParams(vmem_limit_bytes=20 * 1024 * 1024),
    )(lines, panels)
    return out.reshape(matrix.shape)


def solution(mesh):
    in_specs = (P(None, "prow", None, None, "pcol", None), P())
    out_specs = P(None, "prow", None, None, "pcol", None)
    return jax.shard_map(
        functools.partial(per_device, mesh.shape["prow"], mesh.shape["pcol"]),
        mesh=mesh, in_specs=in_specs, out_specs=out_specs, check_vma=False,
    )
```

```python
import functools

import jax
import jax.numpy as jnp
from jax import lax
from jax.experimental import pallas as pl
from jax.experimental.pallas import tpu as pltpu
from jax.sharding import PartitionSpec as P

STEPS = 3
SUB = 2
WINDOW = 8
LAG = 8
BEHIND = LAG + SUB + 1
BACK = 8
DEEP = 4
MESH = pl.DeviceIdType.MESH
BF = jnp.bfloat16
F32 = jnp.float32


def split(value):
    high = value.astype(BF)
    return high, (value - high.astype(F32)).astype(BF)


def left(value):
    high, low = split(value)
    return jnp.concatenate([high, high, low], axis=1)


def right(value):
    high, low = split(value)
    return jnp.concatenate([high, low, high], axis=0)


def dot(a, b):
    return lax.dot_general(a, b, (((1,), (0,)), ((), ())), preferred_element_type=F32)


def gather(
    n_prow, n_pcol, rb, cb, nb, done,
    a_hbm, inv_ref, panels,
    xch, sbuf, abuf, cst, ccol, prow_l,
    rsem, ssem, xrsem, xssem, srcsem, asem,
):
    p = lax.axis_index("prow")
    q = lax.axis_index("pcol")
    depth = n_pcol // 4
    z, x, c = q // 4, (q // 2) % 2, q % 2
    sib = q + 1 - 2 * c
    xn = q + 2 - 4 * x
    sub = nb // SUB
    quarter = sub // 4
    chunks = rb * SUB
    lines = nb * cb * 2
    sub_lines = sub * cb * 2
    stride = cb * 2
    slots = 2 + cb
    inner = ccol.shape[0]
    level = min(n_pcol // n_prow, rb)
    last = rb - level

    barrier = pltpu.get_barrier_semaphore()

    def greet(pp, qq):
        pl.semaphore_signal(barrier, inc=1, device_id=(pp, qq), device_id_type=MESH)

    greet(p, sib)
    greet(p, xn)
    pl.when(z > 0)(lambda: greet(p, q - 4))
    pl.when(z < depth - 1)(lambda: greet(p, q + 4))
    for d in range(1, n_prow):
        greet((p + d) % n_prow, q)
    peers = 1 + n_prow + (z > 0).astype(jnp.int32) + (z < depth - 1).astype(jnp.int32)

    def swap(a):
        if level < 3:
            return a
        return jnp.where(a == last + 1, last + 2, jnp.where(a == last + 2, last + 1, a))

    def place(i):
        return jnp.where(i < last, i, swap(rb - 1 + last - i))

    def chunk(n):
        return place(n // SUB) * SUB + n % SUB

    def block_row(n):
        return place(n // SUB) * n_prow + p

    def near(n):
        return block_row(n) < 4

    def far(n):
        return block_row(n) >= 4

    def have(n, zz):
        g = block_row(n)
        return (g == 1) | (g == 2) | (g >= 4 * zz)

    def rows(n, first, count):
        return pl.ds(pl.multiple_of(chunk(n) * sub + first, quarter), count)

    def remote(ref, n, dev, si, ri):
        return pltpu.make_async_remote_copy(
            src_ref=ref, dst_ref=ref, send_sem=ssem.at[n % WINDOW, si], recv_sem=rsem.at[n, ri],
            device_id=(p, dev), device_id_type=MESH,
        )

    def cp_q(n, count, j, dev, si, ri):
        return remote(panels.at[pl.ds(0, count), rows(n, j * quarter, quarter), :], n, dev, si, ri)

    def cp_k(n, k, dev, si):
        return remote(panels.at[k, rows(n, 0, sub), :], n, dev, si, k)

    def cp_half(n, k, dev, si):
        return remote(panels.at[k, rows(n, sub // 2, sub // 2), :], n, dev, si, k)

    def either(when, yes, no, needed):
        def act(method, n):
            pl.when(needed(n) & when(n))(lambda: getattr(yes(n), method)())
            pl.when(needed(n) & jnp.logical_not(when(n)))(lambda: getattr(no(n), method)())
        return act

    def only(copy, needed):
        return lambda method, n: pl.when(needed(n))(lambda: getattr(copy(n), method)())

    def start(act, n):
        pl.when(n >= WINDOW)(lambda: act("wait_send", n - WINDOW))
        act("start", n)

    def drain(act):
        for n in range(max(chunks - WINDOW, 0), chunks):
            act("wait_send", jnp.int32(n))

    def always(n):
        return n >= 0

    def here(n):
        return have(n, z)

    def beyond(n):
        return have(n, z + 1)

    mine = 2 * x + c
    other = 2 * (1 - x) + c
    up = jnp.minimum(q + 4, n_pcol - 1)

    def quarters(j, dev, si, needed):
        return either(near, lambda n: cp_q(n, 2, j, dev, si, si), lambda n: cp_q(n, STEPS, j, dev, si, si), needed)

    z_out = quarters(mine, up, 0, beyond)
    x_out = quarters(mine, xn, 1, here)
    c1_out = quarters(mine, sib, 2, here)
    c2_out = quarters(other, sib, 3, here)
    z_in = quarters(mine, sib, 0, here)
    x_in = quarters(other, sib, 1, here)
    c1_in = quarters(2 * x + 1 - c, sib, 2, here)
    c2_in = quarters(2 * (1 - x) + 1 - c, sib, 3, here)

    low = (z == 0) & (x == 1)
    above = (z == 1) & (x == 1)

    def two(j, dev, si, ri):
        return only(lambda n: cp_q(n, 2, j, dev, si, ri), far)

    dn_out = two(c, jnp.maximum(q - 4, 0), 4, 3)
    dn_in = two(c, sib, 4, 3)
    dc_out = two(c, sib, 7, 4)
    dc_in = two(1 - c, sib, 7, 4)

    def hop(k, dev):
        whole = lambda n: cp_k(n, k, dev, 1 + 2 * k)
        if k < 2:
            return either(near, whole, lambda n: cp_half(n, k, dev, 1 + 2 * k), always)
        return only(whole, always)

    def to_x(k):
        return hop(k, xn)

    def to_sib(k):
        return only(lambda n: cp_k(n, k, sib, 2 + 2 * k), always)

    def fwd(k):
        return hop(k, sib)

    def fwd_of(k):
        return k + 2 - 4 * ((k // 2) % 2)

    def block_of(slot):
        return slot + 1 if slot < 2 else (slot - 2) * n_pcol + q

    def depth_of(slot):
        return min(slot + 1, STEPS)

    def used(slot):
        return block_of(slot) >= (0 if slot < 2 else STEPS)

    def cp_x(slot, n, part, d):
        return pltpu.make_async_remote_copy(
            src_ref=panels.at[pl.ds(0, depth_of(slot)), rows(n, 0, sub), :],
            dst_ref=xch.at[slot, pl.ds(0, depth_of(slot)), pl.ds(part * sub, sub), :],
            send_sem=xssem.at[slot, part, d], recv_sem=xrsem.at[slot, part],
            device_id=((p + d) % n_prow, q), device_id_type=MESH,
        )

    def cp_l(slot, n, part):
        return pltpu.make_async_copy(
            panels.at[pl.ds(0, depth_of(slot)), rows(n, 0, sub), :],
            xch.at[slot, pl.ds(0, depth_of(slot)), pl.ds(part * sub, sub), :], xrsem.at[slot, part])

    def publish(n):
        for slot in range(slots):
            g = block_of(slot)
            for part in range(SUB):
                @pl.when(used(slot) & (g % n_prow == p) & ((g // n_prow) * SUB + part == chunk(n)))
                def _():
                    for d in range(1, n_prow):
                        cp_x(slot, n, part, d).start()
                    cp_l(slot, n, part).start()

    def wait_slot(slot):
        g = block_of(slot)

        @pl.when(used(slot) & (g % n_prow == p))
        def _():
            for part in range(SUB):
                cp_l(slot, 0, part).wait()

        @pl.when(used(slot) & (g % n_prow != p))
        def _():
            for part in range(SUB):
                cp_x(slot, 0, part, 1).wait_recv()

    def settle(slot):
        @pl.when(used(slot) & (block_of(slot) % n_prow == p))
        def _():
            for part in range(SUB):
                for d in range(1, n_prow):
                    cp_x(slot, 0, part, d).wait_send()

    def a_in(i):
        return pltpu.make_async_copy(
            a_hbm.at[pl.ds(pl.multiple_of(i * lines, lines), lines), :], abuf.at[i % 2], asem.at[i % 2])

    def s_in(n):
        return pltpu.make_async_copy(
            a_hbm.at[pl.ds(pl.multiple_of(chunk(n) * sub_lines, sub_lines), sub_lines), :],
            sbuf.at[n % 2], srcsem.at[n % 2])

    @pl.when(q < STEPS)
    def _():
        s_in(jnp.int32(0)).start()

    if done > 0:
        a_in(jnp.int32(0)).start()
    pl.semaphore_wait(barrier, peers)

    def factor(k, m):
        return cst[k, m * 3 * nb:(m + 1) * 3 * nb, :]

    def factors():
        def mul(u, v):
            return dot(left(u), right(v))

        r00, r11, r22 = inv_ref[0].T, inv_ref[1].T, inv_ref[2].T
        w10 = mul(xch[0, 0], r00)
        w20 = mul(xch[1, 0], r00)
        r01 = -mul(mul(r00, w10.T), r11)
        w21 = mul(xch[1, 0], r01) + mul(xch[1, 1], r11)
        r02 = -mul(mul(r00, w20.T) + mul(r01, w21.T), r22)
        r12 = -mul(mul(r11, w21.T), r22)
        for k, column in enumerate(((r00,), (r01, r11), (r02, r12, r22))):
            for m, value in enumerate(column):
                cst[k, m * 3 * nb:(m + 1) * 3 * nb, :] = right(value)

    def keep(b, m, value):
        panels[m, (rb + b) * nb:(rb + b + 1) * nb, :] = value
        if b < inner:
            ccol[b, m * 3 * nb:(m + 1) * 3 * nb, :] = right(value)

    def columns(b, gb):
        @pl.when(gb >= STEPS)
        def _():
            raw = jnp.concatenate([left(xch[2 + b, m]) for m in range(STEPS)], axis=1)
            solved = [
                right(dot(raw[:, :(k + 1) * 3 * nb], cst[k, :(k + 1) * 3 * nb, :]).T) for k in range(STEPS)]
            for m in range(STEPS):
                total = jnp.zeros((nb, nb), F32)
                for k in range(m, STEPS):
                    f = factor(k, m)
                    total += dot(jnp.concatenate([f[:nb], f[:nb], f[nb:2 * nb]], axis=1), solved[k])
                keep(b, m, total)

        if b == 0:
            for k in range(STEPS):
                @pl.when(gb == k)
                def _():
                    for m in range(STEPS):
                        if m <= k:
                            f = factor(k, m)
                            value = -(f[:nb].astype(F32) + f[nb:2 * nb].astype(F32))
                        else:
                            value = jnp.zeros((nb, nb), F32)
                        keep(b, m, value)

    def ready(g):
        a = g // n_prow
        i = jnp.where(a < last, a, rb - 1 + last - swap(a))
        return i * SUB + SUB - 1

    def tables(t):
        first = jnp.maximum(ready(jnp.int32(1)), ready(jnp.int32(2)))

        @pl.when(t == first)
        def _():
            for slot in range(2):
                wait_slot(slot)
                settle(slot)
            factors()

        for b in range(cb):
            gb = block_of(2 + b)

            @pl.when(t == jnp.maximum(ready(gb), first))
            def _():
                wait_slot(2 + b)
                settle(2 + b)
                columns(b, gb)

    def block(a, g, b):
        gb = block_of(2 + b)
        place_of = pl.ds(pl.multiple_of(a * nb, nb), nb)

        def product():
            return dot(prow_l[...], ccol[b])

        def updated():
            old = jnp.concatenate(
                [abuf[a % 2, pl.ds(b * 2 + h, nb, stride=stride), :] for h in range(2)], axis=1)
            return old - product()

        @pl.when((gb >= STEPS) & (g > gb))
        def _():
            panels[b, place_of, :] = updated()

        @pl.when((gb >= STEPS) & (g == gb))
        def _():
            down = lax.broadcasted_iota(jnp.int32, (nb, nb), 0)
            across = lax.broadcasted_iota(jnp.int32, (nb, nb), 1)
            panels[b, place_of, :] = jnp.where(down >= across, updated(), 0.0)

        if b == 0:
            @pl.when((gb < STEPS) & (g >= gb))
            def _():
                panels[b, place_of, :] = -product()

    def compute(u):
        a = u // SUB
        g = a * n_prow + p

        @pl.when(u % SUB == 0)
        def _():
            @pl.when(a + 1 < done)
            def _():
                a_in(a + 1).start()

            @pl.when(g >= q)
            def _():
                for k in range(STEPS):
                    prow_l[:, k * 3 * nb:(k + 1) * 3 * nb] = left(
                        panels[k, pl.ds(pl.multiple_of(a * nb, nb), nb), :])
            a_in(a).wait()
            block(a, g, 0)

        @pl.when(u % SUB == SUB - 1)
        def _():
            for b in range(1, inner):
                block(a, g, b)

    def step(t, carry):
        @pl.when(t < chunks)
        def _():
            n = t

            @pl.when(z > 0)
            def _():
                z_in("wait_recv", n)
                pl.when(z < depth - 1)(lambda: start(z_out, n))
                start(x_out, n)
                start(c1_out, n)

            for k in range(STEPS):
                @pl.when(q == k)
                def _():
                    s_in(n).wait()

                    @pl.when(n + 1 < chunks)
                    def _():
                        s_in(n + 1).start()
                    for h in range(2):
                        panels[k, rows(n, 0, sub), h * 128:(h + 1) * 128] = sbuf[n % 2, pl.ds(h, sub, stride=stride), :]
                    start(to_x(k), n)
                    start(to_sib(k), n)

        @pl.when((t >= 2) & (t < chunks + 2))
        def _():
            n = t - 2

            @pl.when(z > 0)
            def _():
                x_in("wait_recv", n)
                start(c2_out, n)

            pl.when(above)(lambda: start(dn_out, n))

            for k in range(STEPS):
                @pl.when(q == fwd_of(k))
                def _():
                    fwd(k)("wait_recv", n)
                    start(fwd(k), n)

        @pl.when((t >= 3) & (t < chunks + 3))
        def _():
            n = t - 3

            @pl.when(z > 0)
            def _():
                c1_in("wait_recv", n)
                c2_in("wait_recv", n)

            @pl.when(z == 0)
            def _():
                for k in range(STEPS):
                    same = k + 1 - 2 * (k % 2)

                    @pl.when(q == same)
                    def _():
                        to_sib(k)("wait_recv", n)

                    @pl.when((q != k) & (q != same) & (q != fwd_of(k)))
                    def _():
                        fwd(k)("wait_recv", n)
                start(z_out, n)

            pl.when(jnp.logical_not(low) & ((z == 0) | here(n)))(lambda: publish(n))

        @pl.when(low & (t >= 3 + BACK) & (t < chunks + 3 + BACK))
        def _():
            n = t - 3 - BACK
            dn_in("wait_recv", n)
            start(dc_out, n)

        @pl.when(low & (t >= 4 + BACK) & (t < chunks + 4 + BACK))
        def _():
            n = t - 4 - BACK
            dc_in("wait_recv", n)
            publish(n)

        tables(t - lag)

        u = t - lag + LAG - BEHIND
        pl.when((u >= 0) & (u < done * SUB))(lambda: compute(u))
        return carry

    lag = jnp.where(low, 4 + BACK + LAG, 3 + LAG)
    lax.fori_loop(0, chunks + 4 + BACK + LAG, step, 0)

    pl.when(z < depth - 1)(lambda: drain(z_out))

    @pl.when(z > 0)
    def _():
        drain(x_out)
        drain(c1_out)
        drain(c2_out)

    pl.when(above)(lambda: drain(dn_out))
    pl.when(low)(lambda: drain(dc_out))

    for k in range(STEPS):
        @pl.when(q == k)
        def _():
            drain(to_x(k))
            drain(to_sib(k))

        @pl.when(q == fwd_of(k))
        def _():
            drain(fwd(k))


def update(n_prow, n_pcol, rb, cb, nb, done, a_hbm, panels, out_hbm, abuf, obuf, ccol, prow_l, asem, osem):
    p = lax.axis_index("prow")
    q = lax.axis_index("pcol")
    lines = nb * cb * 2
    stride = cb * 2
    heavy = rb - done
    full = cb - 1 if done == rb - min(n_pcol // n_prow, rb) else 0

    def span(a):
        return pl.ds(pl.multiple_of(a * lines, lines), lines)

    def a_in(j):
        return pltpu.make_async_copy(a_hbm.at[span(done + j), :], abuf.at[j % 2], asem.at[j % 2])

    def o_out(n, a):
        return pltpu.make_async_copy(obuf.at[n % DEEP], out_hbm.at[span(a), :], osem.at[n % DEEP])

    def put(n, b, value):
        for h in range(2):
            obuf[n % DEEP, pl.ds(b * 2 + h, nb, stride=stride), :] = value[:, h * 128:(h + 1) * 128]

    def old(j, b):
        return jnp.concatenate(
            [abuf[j % 2, pl.ds(b * 2 + h, nb, stride=stride), :] for h in range(2)], axis=1)

    def raw(k, a):
        return panels[k, pl.ds(pl.multiple_of(a * nb, nb), nb), :]

    def turn(n):
        @pl.when(n >= DEEP)
        def _():
            o_out(n - DEEP, 0).wait()

    def light(a, n):
        turn(n)
        g = a * n_prow + p
        for b in range(cb):
            gb = b * n_pcol + q
            if b < STEPS:
                pl.when(g >= gb)(lambda: put(n, b, raw(b, a)))
            pl.when((g < gb) | (b >= STEPS))(lambda: put(n, b, jnp.zeros((nb, nb), F32)))
        o_out(n, a).start()

    def dense(j, n, b, product):
        @pl.when(b * n_pcol + q >= STEPS)
        def _():
            put(n, b, old(j, b) - product)

        if b == 0:
            @pl.when(q < STEPS)
            def _():
                put(n, b, -product)

    def block(j, n, g, b):
        gb = b * n_pcol + q

        @pl.when(g > gb)
        def _():
            dense(j, n, b, dot(prow_l[...], ccol[:, b * nb:(b + 1) * nb]))

        @pl.when(g == gb)
        def _():
            product = dot(prow_l[...], ccol[:, b * nb:(b + 1) * nb])
            if b == 0:
                pl.when(q < STEPS)(lambda: put(n, b, -product))

            @pl.when(gb >= STEPS)
            def _():
                down = lax.broadcasted_iota(jnp.int32, (nb, nb), 0)
                across = lax.broadcasted_iota(jnp.int32, (nb, nb), 1)
                put(n, b, jnp.where(down >= across, old(j, b) - product, 0.0))

        @pl.when(g < gb)
        def _():
            put(n, b, jnp.zeros((nb, nb), F32))

    a_in(0).start()
    if heavy > 1:
        a_in(1).start()
    for b in range(cb):
        for m in range(STEPS):
            ccol[m * 3 * nb:(m + 1) * 3 * nb, b * nb:(b + 1) * nb] = right(panels[m, (rb + b) * nb:(rb + b + 1) * nb, :])

    def step(j, carry):
        lo, hi = j * done // heavy, (j + 1) * done // heavy

        def one(a, inner):
            light(a, a + j)
            return inner

        lax.fori_loop(lo, hi, one, 0)
        a, n = done + j, hi + j
        g = a * n_prow + p
        turn(n)
        for k in range(STEPS):
            prow_l[:, k * 3 * nb:(k + 1) * 3 * nb] = left(raw(k, a))
        a_in(j).wait()
        if full:
            product = dot(prow_l[...], ccol[:, :full * nb])
            for b in range(full):
                value = product[:, b * nb:(b + 1) * nb]
                put(n, b, (jnp.where(q < STEPS, 0.0, old(j, b)) if b == 0 else old(j, b)) - value)
        for b in range(full, cb):
            block(j, n, g, b)
        o_out(n, a).start()

        @pl.when(j + 2 < heavy)
        def _():
            a_in(j + 2).start()
        return carry

    lax.fori_loop(0, heavy, step, 0)
    for n in range(max(rb - DEEP, 0), rb):
        o_out(n, 0).wait()


def per_device(n_prow, n_pcol, matrix, inverses):
    rb, _, nb, cb, _, _ = matrix.shape
    lines = matrix.reshape(rb * nb * cb * 2, nb // 2)
    level = min(n_pcol // n_prow, rb)
    done = max(min(rb - max(level, WINDOW // SUB), STEPS * level), 0)
    vmem = pltpu.VMEM
    dma = pltpu.SemaphoreType.DMA
    anywhere = pl.BlockSpec(memory_space=pl.ANY)
    inside = pl.BlockSpec(memory_space=pltpu.VMEM)
    panels = pl.pallas_call(
        functools.partial(gather, n_prow, n_pcol, rb, cb, nb, done),
        out_shape=vmem((STEPS, (rb + cb) * nb, nb), F32),
        in_specs=[anywhere, inside],
        out_specs=inside,
        scratch_shapes=[
            vmem((2 + cb, STEPS, nb, nb), F32),
            vmem((2, nb // SUB * cb * 2, 128), F32),
            vmem((2, nb * cb * 2, 128), F32),
            vmem((STEPS, 3 * STEPS * nb, nb), BF),
            vmem((min(cb, STEPS), 3 * STEPS * nb, nb), BF),
            vmem((nb, 3 * STEPS * nb), BF),
            dma((rb * SUB, 5)),
            dma((WINDOW, 8)),
            dma((2 + cb, SUB)),
            dma((2 + cb, SUB, n_prow)),
            dma((2,)),
            dma((2,)),
        ],
        compiler_params=pltpu.CompilerParams(
            collective_id=0, has_side_effects=True, vmem_limit_bytes=20 * 1024 * 1024
        ),
    )(lines, inverses)
    out = pl.pallas_call(
        functools.partial(update, n_prow, n_pcol, rb, cb, nb, done),
        out_shape=jax.ShapeDtypeStruct(lines.shape, F32),
        in_specs=[anywhere, inside],
        out_specs=anywhere,
        scratch_shapes=[
            vmem((2, nb * cb * 2, 128), F32),
            vmem((DEEP, nb * cb * 2, 128), F32),
            vmem((3 * STEPS * nb, cb * nb), BF),
            vmem((nb, 3 * STEPS * nb), BF),
            dma((2,)),
            dma((DEEP,)),
        ],
        compiler_params=pltpu.CompilerParams(vmem_limit_bytes=24 * 1024 * 1024),
    )(lines, panels)
    return out.reshape(matrix.shape)


def solution(mesh):
    in_specs = (P(None, "prow", None, None, "pcol", None), P())
    out_specs = P(None, "prow", None, None, "pcol", None)
    return jax.shard_map(
        functools.partial(per_device, mesh.shape["prow"], mesh.shape["pcol"]),
        mesh=mesh, in_specs=in_specs, out_specs=out_specs, check_vma=False,
    )
```

```python
import functools
import types

import jax
import jax.numpy as jnp
from jax import lax
from jax.experimental import pallas as pl
from jax.experimental.pallas import tpu as pltpu
from jax.sharding import PartitionSpec as P

STEPS = 3
SUB = 2
WINDOW = 8
LAG = 8
AHEAD = 4
HOP = 3
FULL = 4
PAIR = 1
BACK = 11
DEEP = 6
MESH = pl.DeviceIdType.MESH
BF = jnp.bfloat16
F32 = jnp.float32


def split(value):
    high = value.astype(BF)
    return high, (value - high.astype(F32)).astype(BF)


def left(value):
    high, low = split(value)
    return jnp.concatenate([high, high, low], axis=1)


def right(value):
    high, low = split(value)
    return jnp.concatenate([high, low, high], axis=0)


def dot(a, b):
    return lax.dot_general(a, b, (((1,), (0,)), ((), ())), preferred_element_type=F32)


def gather(
    n_prow, n_pcol, rb, cb, nb, done,
    a_hbm, inv_ref, panels,
    xch, sbuf, abuf, cst, ccol, prow_l,
    rsem, ssem, xrsem, xssem, srcsem, asem,
):
    p = lax.axis_index("prow")
    q = lax.axis_index("pcol")
    depth = n_pcol // 4
    z, x, c = q // 4, (q // 2) % 2, q % 2
    sib = q + 1 - 2 * c
    xn = q + 2 - 4 * x
    sub = nb // SUB
    quarter = sub // 4
    chunks = rb * SUB
    lines = nb * cb * 2
    sub_lines = sub * cb * 2
    stride = cb * 2
    slots = 2 + cb
    inner = ccol.shape[0]
    level = min(n_pcol // n_prow, rb)
    last = rb - level
    first_level = min(level, last)
    early = 3 // n_prow + 1
    behind = LAG + SUB * level
    down = FULL + BACK

    barrier = pltpu.get_barrier_semaphore()

    def greet(pp, qq):
        pl.semaphore_signal(barrier, inc=1, device_id=(pp, qq), device_id_type=MESH)

    greet(p, sib)
    greet(p, xn)
    pl.when(z > 0)(lambda: greet(p, q - 4))
    pl.when(z < depth - 1)(lambda: greet(p, q + 4))
    for d in range(1, n_prow):
        greet((p + d) % n_prow, q)
    peers = 1 + n_prow + (z > 0).astype(jnp.int32) + (z < depth - 1).astype(jnp.int32)

    def swap(a):
        if level < 3:
            return a
        return jnp.where(a == last + 1, last + 2, jnp.where(a == last + 2, last + 1, a))

    def place(i):
        turned = i + early % max(first_level, 1)
        a = jnp.where(i < first_level, jnp.where(turned >= first_level, turned - first_level, turned), i)
        return jnp.where(i < last, a, swap(rb - 1 + last - i))

    def spot(n):
        i = lax.div(n, SUB)
        part = n - i * SUB
        a = place(i)
        g = a * n_prow + p
        live = n >= 0
        seed = (g == 1) | (g == 2)
        here = live & (seed | (g >= 4 * z))
        beyond = live & (seed | (g >= 4 * (z + 1)))
        near = g < 4
        return types.SimpleNamespace(
            n=n, part=part, a=a, line=a * SUB + part, row=(a * SUB + part) * sub, slot=lax.rem(n, WINDOW),
            live=(live & near, live & jnp.logical_not(near)), here=(here & near, here & jnp.logical_not(near)),
            beyond=(beyond & near, beyond & jnp.logical_not(near)), kept=here, always=live)

    def rows(s, first, count):
        return pl.ds(pl.multiple_of(s.row + first, quarter), count)

    def remote(ref, s, dev, si, ri):
        return pltpu.make_async_remote_copy(
            src_ref=ref, dst_ref=ref, send_sem=ssem.at[s.slot, si], recv_sem=rsem.at[s.n, ri],
            device_id=(p, dev), device_id_type=MESH,
        )

    def cp_q(s, count, j, dev, si, ri):
        return remote(panels.at[pl.ds(0, count), rows(s, j * quarter, quarter), :], s, dev, si, ri)

    def cp_k(s, k, dev, si):
        return remote(panels.at[k, rows(s, 0, sub), :], s, dev, si, k)

    def cp_half(s, k, dev, si):
        return remote(panels.at[k, rows(s, sub // 2, sub // 2), :], s, dev, si, k)

    def either(yes, no, needed):
        def act(method, s):
            near, far = getattr(s, needed)
            pl.when(near)(lambda: getattr(yes(s), method)())
            pl.when(far)(lambda: getattr(no(s), method)())
        return act

    def start(act, s, w):
        act("wait_send", w)
        act("start", s)

    def drain(act):
        for n in range(max(chunks - WINDOW, 0), chunks):
            act("wait_send", spot(jnp.int32(n)))

    mine = 2 * x + c
    other = 2 * (1 - x) + c
    up = jnp.minimum(q + 4, n_pcol - 1)

    def quarters(j, dev, si, needed):
        return either(lambda s: cp_q(s, 2, j, dev, si, si), lambda s: cp_q(s, STEPS, j, dev, si, si), needed)

    z_out = quarters(mine, up, 0, "beyond")
    x_out = quarters(mine, xn, 1, "here")
    c1_out = quarters(mine, sib, 2, "here")
    c2_out = quarters(other, sib, 3, "here")
    z_in = quarters(mine, sib, 0, "here")
    x_in = quarters(other, sib, 1, "here")
    c1_in = quarters(2 * x + 1 - c, sib, 2, "here")
    c2_in = quarters(2 * (1 - x) + 1 - c, sib, 3, "here")

    low = (z == 0) & (x == 1)
    above = (z == 1) & (x == 1)

    def two(j, dev, si, ri):
        return lambda method, s: pl.when(s.live[1])(lambda: getattr(cp_q(s, 2, j, dev, si, ri), method)())

    dn_out = two(c, jnp.maximum(q - 4, 0), 4, 3)
    dn_in = two(c, sib, 4, 3)
    dc_out = two(c, sib, 7, 4)
    dc_in = two(1 - c, sib, 7, 4)

    def whole(k, dev, si):
        return lambda method, s: pl.when(s.always)(lambda: getattr(cp_k(s, k, dev, si), method)())

    def hop(k, dev):
        if k < 2:
            return either(
                lambda s: cp_k(s, k, dev, 1 + 2 * k), lambda s: cp_half(s, k, dev, 1 + 2 * k), "live")
        return whole(k, dev, 1 + 2 * k)

    def to_x(k):
        return hop(k, xn)

    def to_sib(k):
        return whole(k, sib, 2 + 2 * k)

    def fwd(k):
        return hop(k, sib)

    def fwd_of(k):
        return k + 2 - 4 * ((k // 2) % 2)

    def block_of(slot):
        return slot + 1 if slot < 2 else (slot - 2) * n_pcol + q

    def depth_of(slot):
        return min(slot + 1, STEPS)

    def used(slot):
        return block_of(slot) >= (0 if slot < 2 else STEPS)

    def cp_x(slot, s, part, d):
        return pltpu.make_async_remote_copy(
            src_ref=panels.at[pl.ds(0, depth_of(slot)), rows(s, 0, sub), :],
            dst_ref=xch.at[slot, pl.ds(0, depth_of(slot)), pl.ds(part * sub, sub), :],
            send_sem=xssem.at[slot, part, d], recv_sem=xrsem.at[slot, part],
            device_id=((p + d) % n_prow, q), device_id_type=MESH,
        )

    def cp_l(slot, s, part):
        return pltpu.make_async_copy(
            panels.at[pl.ds(0, depth_of(slot)), rows(s, 0, sub), :],
            xch.at[slot, pl.ds(0, depth_of(slot)), pl.ds(part * sub, sub), :], xrsem.at[slot, part])

    owned = [used(slot) & (block_of(slot) % n_prow == p) for slot in range(slots)]
    taken = [used(slot) & (block_of(slot) % n_prow != p) for slot in range(slots)]
    owner = [block_of(slot) // n_prow for slot in range(slots)]
    zero = spot(jnp.int32(0))

    def publish(s, wanted):
        for slot in range(slots):
            @pl.when(wanted & owned[slot] & (owner[slot] == s.a))
            def _():
                for d in range(1, n_prow):
                    cp_x(slot, s, s.part, d).start()
                cp_l(slot, s, s.part).start()

    def wait_slot(slot):
        @pl.when(owned[slot])
        def _():
            for part in range(SUB):
                cp_l(slot, zero, part).wait()

        @pl.when(taken[slot])
        def _():
            for part in range(SUB):
                cp_x(slot, zero, part, 1).wait_recv()

    def settle(slot):
        @pl.when(owned[slot])
        def _():
            for part in range(SUB):
                for d in range(1, n_prow):
                    cp_x(slot, zero, part, d).wait_send()

    def a_in(i):
        return pltpu.make_async_copy(
            a_hbm.at[pl.ds(pl.multiple_of(place(i) * lines, lines), lines), :], abuf.at[i % 2], asem.at[i % 2])

    def s_in(s):
        ahead = lax.rem(s.n, AHEAD)
        return pltpu.make_async_copy(
            a_hbm.at[pl.ds(pl.multiple_of(s.line * sub_lines, sub_lines), sub_lines), :],
            sbuf.at[ahead], srcsem.at[ahead])

    @pl.when(q < STEPS)
    def _():
        for n in range(min(AHEAD, chunks)):
            s_in(spot(jnp.int32(n))).start()

    if done > 0:
        a_in(jnp.int32(0)).start()
    pl.semaphore_wait(barrier, peers)

    def factor(k, m):
        return cst[k, m * 3 * nb:(m + 1) * 3 * nb, :]

    def factors():
        def mul(u, v):
            return dot(left(u), right(v))

        r00, r11, r22 = inv_ref[0].T, inv_ref[1].T, inv_ref[2].T
        w10 = mul(xch[0, 0], r00)
        w20 = mul(xch[1, 0], r00)
        r01 = -mul(mul(r00, w10.T), r11)
        w21 = mul(xch[1, 0], r01) + mul(xch[1, 1], r11)
        r02 = -mul(mul(r00, w20.T) + mul(r01, w21.T), r22)
        r12 = -mul(mul(r11, w21.T), r22)
        for k, column in enumerate(((r00,), (r01, r11), (r02, r12, r22))):
            for m, value in enumerate(column):
                cst[k, m * 3 * nb:(m + 1) * 3 * nb, :] = right(value)

    def keep(b, m, value):
        panels[m, (rb + b) * nb:(rb + b + 1) * nb, :] = value
        if b < inner:
            ccol[b, m * 3 * nb:(m + 1) * 3 * nb, :] = right(value)

    def columns(b, gb):
        @pl.when(gb >= STEPS)
        def _():
            raw = jnp.concatenate([left(xch[2 + b, m]) for m in range(STEPS)], axis=1)
            solved = [
                right(dot(raw[:, :(k + 1) * 3 * nb], cst[k, :(k + 1) * 3 * nb, :]).T) for k in range(STEPS)]
            for m in range(STEPS):
                total = jnp.zeros((nb, nb), F32)
                for k in range(m, STEPS):
                    f = factor(k, m)
                    total += dot(jnp.concatenate([f[:nb], f[:nb], f[nb:2 * nb]], axis=1), solved[k])
                keep(b, m, total)

        if b == 0:
            for k in range(STEPS):
                @pl.when(gb == k)
                def _():
                    for m in range(STEPS):
                        if m <= k:
                            f = factor(k, m)
                            value = -(f[:nb].astype(F32) + f[nb:2 * nb].astype(F32))
                        else:
                            value = jnp.zeros((nb, nb), F32)
                        keep(b, m, value)

    def ready(g):
        a = g // n_prow
        i = jnp.where(a < first_level, (a + first_level * early - early) % max(first_level, 1), a)
        i = jnp.where(a < last, i, rb - 1 + last - swap(a))
        return i * SUB + SUB - 1

    first = jnp.maximum(ready(jnp.int32(1)), ready(jnp.int32(2)))
    when = [jnp.maximum(ready(block_of(2 + b)), first) for b in range(cb)]

    def tables(t):
        @pl.when(t == first)
        def _():
            for slot in range(2):
                wait_slot(slot)
                settle(slot)
            factors()

        for b in range(cb):
            @pl.when(t == when[b])
            def _():
                wait_slot(2 + b)
                settle(2 + b)
                columns(b, block_of(2 + b))

    def block(i, a, g, b):
        gb = block_of(2 + b)
        place_of = pl.ds(pl.multiple_of(a * nb, nb), nb)

        def product():
            return dot(prow_l[...], ccol[b])

        def updated():
            old = jnp.concatenate(
                [abuf[i % 2, pl.ds(b * 2 + h, nb, stride=stride), :] for h in range(2)], axis=1)
            return old - product()

        @pl.when((gb >= STEPS) & (g > gb))
        def _():
            panels[b, place_of, :] = updated()

        @pl.when((gb >= STEPS) & (g == gb))
        def _():
            down = lax.broadcasted_iota(jnp.int32, (nb, nb), 0)
            across = lax.broadcasted_iota(jnp.int32, (nb, nb), 1)
            panels[b, place_of, :] = jnp.where(down >= across, updated(), 0.0)

        if b == 0:
            @pl.when((gb < STEPS) & (g >= gb))
            def _():
                panels[b, place_of, :] = -product()

    def compute(u):
        i = lax.div(u, SUB)
        part = u - i * SUB
        a = place(i)
        g = a * n_prow + p

        @pl.when(part == 0)
        def _():
            @pl.when(i + 1 < done)
            def _():
                a_in(i + 1).start()

            @pl.when(g >= q)
            def _():
                for k in range(STEPS):
                    prow_l[:, k * 3 * nb:(k + 1) * 3 * nb] = left(
                        panels[k, pl.ds(pl.multiple_of(a * nb, nb), nb), :])
            a_in(i).wait()
            block(i, a, g, 0)

        for b in range(1, inner):
            pl.when(part == min(b, SUB - 1))(lambda: block(i, a, g, b))

    def step(t, carry):
        @pl.when(t < chunks)
        def _():
            s, w = spot(t), spot(t - WINDOW)

            @pl.when(z > 0)
            def _():
                z_in("wait_recv", s)
                pl.when(z < depth - 1)(lambda: start(z_out, s, w))
                start(x_out, s, w)
                start(c1_out, s, w)

            for k in range(STEPS):
                @pl.when(q == k)
                def _():
                    s_in(s).wait()
                    ahead = lax.rem(t, AHEAD)
                    for h in range(2):
                        panels[k, rows(s, 0, sub), h * 128:(h + 1) * 128] = sbuf[ahead, pl.ds(h, sub, stride=stride), :]
                    start(to_x(k), s, w)
                    start(to_sib(k), s, w)

                    @pl.when(t + AHEAD < chunks)
                    def _():
                        s_in(spot(t + AHEAD)).start()

        @pl.when((t >= HOP) & (t < chunks + HOP))
        def _():
            s, w = spot(t - HOP), spot(t - HOP - WINDOW)

            @pl.when(z > 0)
            def _():
                x_in("wait_recv", s)
                start(c2_out, s, w)

            pl.when(above)(lambda: start(dn_out, s, w))

            for k in range(STEPS):
                @pl.when(q == fwd_of(k))
                def _():
                    fwd(k)("wait_recv", s)
                    start(fwd(k), s, w)

        @pl.when((t >= FULL) & (t < chunks + FULL))
        def _():
            s = spot(t - FULL)

            @pl.when(z > 0)
            def _():
                c1_in("wait_recv", s)
                c2_in("wait_recv", s)

            @pl.when(z == 0)
            def _():
                for k in range(STEPS):
                    same = k + 1 - 2 * (k % 2)

                    @pl.when(q == same)
                    def _():
                        to_sib(k)("wait_recv", s)

                    @pl.when((q != k) & (q != same) & (q != fwd_of(k)))
                    def _():
                        fwd(k)("wait_recv", s)
                start(z_out, s, spot(t - FULL - WINDOW))

            pl.when(jnp.logical_not(low))(lambda: publish(s, s.kept))

        @pl.when(low & (t >= down) & (t < chunks + down + PAIR))
        def _():
            @pl.when(t < chunks + down)
            def _():
                s = spot(t - down)
                dn_in("wait_recv", s)
                start(dc_out, s, spot(t - down - WINDOW))

            @pl.when(t >= down + PAIR)
            def _():
                s = spot(t - down - PAIR)
                dc_in("wait_recv", s)
                publish(s, s.kept)

        tables(t - lag)

        v = t - lag + LAG - behind
        for extra in range(2):
            u = v + v // 4 + extra
            pl.when((v >= 0) & (u < done * SUB) & (v % 4 >= 3 * extra))(lambda: compute(u))
        return carry

    lag = jnp.where(low, down + PAIR, FULL) + LAG
    lax.fori_loop(0, chunks + down + PAIR + LAG, step, 0)

    pl.when(z < depth - 1)(lambda: drain(z_out))

    @pl.when(z > 0)
    def _():
        drain(x_out)
        drain(c1_out)
        drain(c2_out)

    pl.when(above)(lambda: drain(dn_out))
    pl.when(low)(lambda: drain(dc_out))

    for k in range(STEPS):
        @pl.when(q == k)
        def _():
            drain(to_x(k))
            drain(to_sib(k))

        @pl.when(q == fwd_of(k))
        def _():
            drain(fwd(k))


def update(n_prow, n_pcol, rb, cb, nb, done, a_hbm, panels, out_hbm, abuf, obuf, ccol, prow_l, asem, osem):
    p = lax.axis_index("prow")
    q = lax.axis_index("pcol")
    lines = nb * cb * 2
    stride = cb * 2
    heavy = rb - done
    full = cb - 1 if done == rb - min(n_pcol // n_prow, rb) else 0

    def span(a):
        return pl.ds(pl.multiple_of(a * lines, lines), lines)

    def a_in(j):
        return pltpu.make_async_copy(a_hbm.at[span(done + j), :], abuf.at[j % 2], asem.at[j % 2])

    def o_out(n, a):
        return pltpu.make_async_copy(obuf.at[n % DEEP], out_hbm.at[span(a), :], osem.at[n % DEEP])

    def put(n, b, value):
        for h in range(2):
            obuf[n % DEEP, pl.ds(b * 2 + h, nb, stride=stride), :] = value[:, h * 128:(h + 1) * 128]

    def old(j, b):
        return jnp.concatenate(
            [abuf[j % 2, pl.ds(b * 2 + h, nb, stride=stride), :] for h in range(2)], axis=1)

    def raw(k, a):
        return panels[k, pl.ds(pl.multiple_of(a * nb, nb), nb), :]

    def turn(n):
        @pl.when(n >= DEEP)
        def _():
            o_out(n - DEEP, 0).wait()

    def light(a, n):
        turn(n)
        g = a * n_prow + p
        for b in range(cb):
            gb = b * n_pcol + q
            if b < STEPS:
                pl.when(g >= gb)(lambda: put(n, b, raw(b, a)))
            pl.when((g < gb) | (b >= STEPS))(lambda: put(n, b, jnp.zeros((nb, nb), F32)))
        o_out(n, a).start()

    def dense(j, n, b, product):
        @pl.when(b * n_pcol + q >= STEPS)
        def _():
            put(n, b, old(j, b) - product)

        if b == 0:
            @pl.when(q < STEPS)
            def _():
                put(n, b, -product)

    def block(j, n, g, b):
        gb = b * n_pcol + q

        @pl.when(g > gb)
        def _():
            dense(j, n, b, dot(prow_l[...], ccol[:, b * nb:(b + 1) * nb]))

        @pl.when(g == gb)
        def _():
            product = dot(prow_l[...], ccol[:, b * nb:(b + 1) * nb])
            if b == 0:
                pl.when(q < STEPS)(lambda: put(n, b, -product))

            @pl.when(gb >= STEPS)
            def _():
                down = lax.broadcasted_iota(jnp.int32, (nb, nb), 0)
                across = lax.broadcasted_iota(jnp.int32, (nb, nb), 1)
                put(n, b, jnp.where(down >= across, old(j, b) - product, 0.0))

        @pl.when(g < gb)
        def _():
            put(n, b, jnp.zeros((nb, nb), F32))

    a_in(0).start()
    if heavy > 1:
        a_in(1).start()
    def step(j, carry):
        lo, hi = j * done // heavy, (j + 1) * done // heavy

        def one(a, inner):
            light(a, a + j)
            return inner

        lax.fori_loop(lo, hi, one, 0)

        @pl.when(j == 0)
        def _():
            for b in range(cb):
                for m in range(STEPS):
                    ccol[m * 3 * nb:(m + 1) * 3 * nb, b * nb:(b + 1) * nb] = right(
                        panels[m, (rb + b) * nb:(rb + b + 1) * nb, :])

        a, n = done + j, hi + j
        g = a * n_prow + p
        turn(n)
        for k in range(STEPS):
            prow_l[:, k * 3 * nb:(k + 1) * 3 * nb] = left(raw(k, a))
        a_in(j).wait()
        if full:
            product = dot(prow_l[...], ccol[:, :full * nb])
            for b in range(full):
                value = product[:, b * nb:(b + 1) * nb]
                put(n, b, (jnp.where(q < STEPS, 0.0, old(j, b)) if b == 0 else old(j, b)) - value)
        for b in range(full, cb):
            block(j, n, g, b)
        o_out(n, a).start()

        @pl.when(j + 2 < heavy)
        def _():
            a_in(j + 2).start()
        return carry

    lax.fori_loop(0, heavy, step, 0)
    for n in range(max(rb - DEEP, 0), rb):
        o_out(n, 0).wait()


def per_device(n_prow, n_pcol, matrix, inverses):
    rb, _, nb, cb, _, _ = matrix.shape
    lines = matrix.reshape(rb * nb * cb * 2, nb // 2)
    level = min(n_pcol // n_prow, rb)
    done = max(min(rb - max(level, WINDOW // SUB), STEPS * level), 0)
    vmem = pltpu.VMEM
    dma = pltpu.SemaphoreType.DMA
    anywhere = pl.BlockSpec(memory_space=pl.ANY)
    inside = pl.BlockSpec(memory_space=pltpu.VMEM)
    panels = pl.pallas_call(
        functools.partial(gather, n_prow, n_pcol, rb, cb, nb, done),
        out_shape=vmem((STEPS, (rb + cb) * nb, nb), F32),
        in_specs=[anywhere, inside],
        out_specs=inside,
        scratch_shapes=[
            vmem((2 + cb, STEPS, nb, nb), F32),
            vmem((AHEAD, nb // SUB * cb * 2, 128), F32),
            vmem((2, nb * cb * 2, 128), F32),
            vmem((STEPS, 3 * STEPS * nb, nb), BF),
            vmem((min(cb, STEPS), 3 * STEPS * nb, nb), BF),
            vmem((nb, 3 * STEPS * nb), BF),
            dma((rb * SUB, 5)),
            dma((WINDOW, 8)),
            dma((2 + cb, SUB)),
            dma((2 + cb, SUB, n_prow)),
            dma((AHEAD,)),
            dma((2,)),
        ],
        compiler_params=pltpu.CompilerParams(
            collective_id=0, has_side_effects=True, vmem_limit_bytes=24 * 1024 * 1024
        ),
    )(lines, inverses)
    out = pl.pallas_call(
        functools.partial(update, n_prow, n_pcol, rb, cb, nb, done),
        out_shape=jax.ShapeDtypeStruct(lines.shape, F32),
        in_specs=[anywhere, inside],
        out_specs=anywhere,
        scratch_shapes=[
            vmem((2, nb * cb * 2, 128), F32),
            vmem((DEEP, nb * cb * 2, 128), F32),
            vmem((3 * STEPS * nb, cb * nb), BF),
            vmem((nb, 3 * STEPS * nb), BF),
            dma((2,)),
            dma((DEEP,)),
        ],
        compiler_params=pltpu.CompilerParams(vmem_limit_bytes=24 * 1024 * 1024),
    )(lines, panels)
    return out.reshape(matrix.shape)


def solution(mesh):
    in_specs = (P(None, "prow", None, None, "pcol", None), P())
    out_specs = P(None, "prow", None, None, "pcol", None)
    return jax.shard_map(
        functools.partial(per_device, mesh.shape["prow"], mesh.shape["pcol"]),
        mesh=mesh, in_specs=in_specs, out_specs=out_specs, check_vma=False,
    )
```

```python
import functools
import types

import jax
import jax.numpy as jnp
from jax import lax
from jax.experimental import pallas as pl
from jax.experimental.pallas import tpu as pltpu
from jax.sharding import PartitionSpec as P

STEPS = 3
SUB = 2
WINDOW = 8
LAG = 8
AHEAD = 4
HOP = 3
FULL = 4
PAIR = 1
BACK = 11
DEEP = 6
MESH = pl.DeviceIdType.MESH
BF = jnp.bfloat16
F32 = jnp.float32


def split(value):
    high = value.astype(BF)
    return high, (value - high.astype(F32)).astype(BF)


def left(value):
    high, low = split(value)
    return jnp.concatenate([high, high, low], axis=1)


def right(value):
    high, low = split(value)
    return jnp.concatenate([high, low, high], axis=0)


def dot(a, b):
    return lax.dot_general(a, b, (((1,), (0,)), ((), ())), preferred_element_type=F32)


def gather(
    n_prow, n_pcol, rb, cb, nb, done,
    a_hbm, inv_ref, panels,
    xch, sbuf, abuf, cst, ccol, prow_l,
    rsem, ssem, xrsem, xssem, srcsem, asem,
):
    p = lax.axis_index("prow")
    q = lax.axis_index("pcol")
    depth = n_pcol // 4
    z, x, c = q // 4, (q // 2) % 2, q % 2
    sib = q + 1 - 2 * c
    xn = q + 2 - 4 * x
    sub = nb // SUB
    quarter = sub // 4
    chunks = rb * SUB
    lines = nb * cb * 2
    sub_lines = sub * cb * 2
    stride = cb * 2
    slots = 2 + cb
    inner = ccol.shape[0]
    level = min(n_pcol // n_prow, rb)
    last = rb - level
    first_level = min(level, last)
    early = 3 // n_prow + 1
    behind = LAG + SUB * level
    down = FULL + BACK

    barrier = pltpu.get_barrier_semaphore()

    def greet(pp, qq):
        pl.semaphore_signal(barrier, inc=1, device_id=(pp, qq), device_id_type=MESH)

    greet(p, sib)
    greet(p, xn)
    pl.when(z > 0)(lambda: greet(p, q - 4))
    pl.when(z < depth - 1)(lambda: greet(p, q + 4))
    for d in range(1, n_prow):
        greet((p + d) % n_prow, q)
    peers = 1 + n_prow + (z > 0).astype(jnp.int32) + (z < depth - 1).astype(jnp.int32)

    def swap(a):
        if level < 3:
            return a
        return jnp.where(a == last + 1, last + 2, jnp.where(a == last + 2, last + 1, a))

    def place(i):
        turned = i + early % max(first_level, 1)
        a = jnp.where(i < first_level, jnp.where(turned >= first_level, turned - first_level, turned), i)
        return jnp.where(i < last, a, swap(rb - 1 + last - i))

    def spot(n):
        i = lax.div(n, SUB)
        part = n - i * SUB
        a = place(i)
        g = a * n_prow + p
        live = n >= 0
        seed = (g == 1) | (g == 2)
        here = live & (seed | (g >= 4 * z))
        beyond = live & (seed | (g >= 4 * (z + 1)))
        near = g < 4
        return types.SimpleNamespace(
            n=n, part=part, a=a, line=a * SUB + part, row=(a * SUB + part) * sub, slot=lax.rem(n, WINDOW),
            live=(live & near, live & jnp.logical_not(near)), here=(here & near, here & jnp.logical_not(near)),
            beyond=(beyond & near, beyond & jnp.logical_not(near)), kept=here, always=live)

    def rows(s, first, count):
        return pl.ds(pl.multiple_of(s.row + first, quarter), count)

    def remote(ref, s, dev, si, ri):
        return pltpu.make_async_remote_copy(
            src_ref=ref, dst_ref=ref, send_sem=ssem.at[s.slot, si], recv_sem=rsem.at[s.n, ri],
            device_id=(p, dev), device_id_type=MESH,
        )

    def cp_q(s, count, j, dev, si, ri):
        return remote(panels.at[pl.ds(0, count), rows(s, j * quarter, quarter), :], s, dev, si, ri)

    def cp_k(s, k, dev, si):
        return remote(panels.at[k, rows(s, 0, sub), :], s, dev, si, k)

    def cp_half(s, k, dev, si):
        return remote(panels.at[k, rows(s, sub // 2, sub // 2), :], s, dev, si, k)

    def either(yes, no, needed):
        def act(method, s):
            near, far = getattr(s, needed)
            pl.when(near)(lambda: getattr(yes(s), method)())
            pl.when(far)(lambda: getattr(no(s), method)())
        return act

    def start(act, s, w):
        act("wait_send", w)
        act("start", s)

    def drain(act):
        for n in range(max(chunks - WINDOW, 0), chunks):
            act("wait_send", spot(jnp.int32(n)))

    mine = 2 * x + c
    other = 2 * (1 - x) + c
    up = jnp.minimum(q + 4, n_pcol - 1)

    def quarters(j, dev, si, needed):
        return either(lambda s: cp_q(s, 2, j, dev, si, si), lambda s: cp_q(s, STEPS, j, dev, si, si), needed)

    z_out = quarters(mine, up, 0, "beyond")
    x_out = quarters(mine, xn, 1, "here")
    c1_out = quarters(mine, sib, 2, "here")
    c2_out = quarters(other, sib, 3, "here")
    z_in = quarters(mine, sib, 0, "here")
    x_in = quarters(other, sib, 1, "here")
    c1_in = quarters(2 * x + 1 - c, sib, 2, "here")
    c2_in = quarters(2 * (1 - x) + 1 - c, sib, 3, "here")

    low = (z == 0) & (x == 1)
    above = (z == 1) & (x == 1)

    def two(j, dev, si, ri):
        return lambda method, s: pl.when(s.live[1])(lambda: getattr(cp_q(s, 2, j, dev, si, ri), method)())

    dn_out = two(c, jnp.maximum(q - 4, 0), 4, 3)
    dn_in = two(c, sib, 4, 3)
    dc_out = two(c, sib, 7, 4)
    dc_in = two(1 - c, sib, 7, 4)

    def whole(k, dev, si):
        return lambda method, s: pl.when(s.always)(lambda: getattr(cp_k(s, k, dev, si), method)())

    def hop(k, dev):
        if k < 2:
            return either(
                lambda s: cp_k(s, k, dev, 1 + 2 * k), lambda s: cp_half(s, k, dev, 1 + 2 * k), "live")
        return whole(k, dev, 1 + 2 * k)

    def to_x(k):
        return hop(k, xn)

    def to_sib(k):
        return whole(k, sib, 2 + 2 * k)

    def fwd(k):
        return hop(k, sib)

    def fwd_of(k):
        return k + 2 - 4 * ((k // 2) % 2)

    def block_of(slot):
        return slot + 1 if slot < 2 else (slot - 2) * n_pcol + q

    def depth_of(slot):
        return min(slot + 1, STEPS)

    def used(slot):
        return block_of(slot) >= (0 if slot < 2 else STEPS)

    def cp_x(slot, s, part, d):
        return pltpu.make_async_remote_copy(
            src_ref=panels.at[pl.ds(0, depth_of(slot)), rows(s, 0, sub), :],
            dst_ref=xch.at[slot, pl.ds(0, depth_of(slot)), pl.ds(part * sub, sub), :],
            send_sem=xssem.at[slot, part, d], recv_sem=xrsem.at[slot, part],
            device_id=((p + d) % n_prow, q), device_id_type=MESH,
        )

    def cp_l(slot, s, part):
        return pltpu.make_async_copy(
            panels.at[pl.ds(0, depth_of(slot)), rows(s, 0, sub), :],
            xch.at[slot, pl.ds(0, depth_of(slot)), pl.ds(part * sub, sub), :], xrsem.at[slot, part])

    owned = [used(slot) & (block_of(slot) % n_prow == p) for slot in range(slots)]
    taken = [used(slot) & (block_of(slot) % n_prow != p) for slot in range(slots)]
    owner = [block_of(slot) // n_prow for slot in range(slots)]
    zero = spot(jnp.int32(0))

    def publish(s, wanted):
        for slot in range(slots):
            @pl.when(wanted & owned[slot] & (owner[slot] == s.a))
            def _():
                for d in range(1, n_prow):
                    cp_x(slot, s, s.part, d).start()
                cp_l(slot, s, s.part).start()

    def wait_slot(slot):
        @pl.when(owned[slot])
        def _():
            for part in range(SUB):
                cp_l(slot, zero, part).wait()

        @pl.when(taken[slot])
        def _():
            for part in range(SUB):
                cp_x(slot, zero, part, 1).wait_recv()

    def settle(slot):
        @pl.when(owned[slot])
        def _():
            for part in range(SUB):
                for d in range(1, n_prow):
                    cp_x(slot, zero, part, d).wait_send()

    def a_in(i):
        return pltpu.make_async_copy(
            a_hbm.at[pl.ds(pl.multiple_of(place(i) * lines, lines), lines), :], abuf.at[i % 2], asem.at[i % 2])

    def s_in(s):
        ahead = lax.rem(s.n, AHEAD)
        return pltpu.make_async_copy(
            a_hbm.at[pl.ds(pl.multiple_of(s.line * sub_lines, sub_lines), sub_lines), :],
            sbuf.at[ahead], srcsem.at[ahead])

    @pl.when(q < STEPS)
    def _():
        for n in range(min(AHEAD, chunks)):
            s_in(spot(jnp.int32(n))).start()

    if done > 0:
        a_in(jnp.int32(0)).start()
    pl.semaphore_wait(barrier, peers)

    def factor(k, m):
        return cst[k, m * 3 * nb:(m + 1) * 3 * nb, :]

    def factors():
        def mul(u, v):
            return dot(left(u), right(v))

        r00, r11, r22 = inv_ref[0].T, inv_ref[1].T, inv_ref[2].T
        w10 = mul(xch[0, 0], r00)
        w20 = mul(xch[1, 0], r00)
        r01 = -mul(mul(r00, w10.T), r11)
        w21 = mul(xch[1, 0], r01) + mul(xch[1, 1], r11)
        r02 = -mul(mul(r00, w20.T) + mul(r01, w21.T), r22)
        r12 = -mul(mul(r11, w21.T), r22)
        for k, column in enumerate(((r00,), (r01, r11), (r02, r12, r22))):
            for m, value in enumerate(column):
                cst[k, m * 3 * nb:(m + 1) * 3 * nb, :] = right(value)

    def keep(b, m, value):
        panels[m, (rb + b) * nb:(rb + b + 1) * nb, :] = value
        if b < inner:
            ccol[b, m * 3 * nb:(m + 1) * 3 * nb, :] = right(value)

    def columns(b, gb):
        @pl.when(gb >= STEPS)
        def _():
            raw = jnp.concatenate([left(xch[2 + b, m]) for m in range(STEPS)], axis=1)
            solved = [
                right(dot(raw[:, :(k + 1) * 3 * nb], cst[k, :(k + 1) * 3 * nb, :]).T) for k in range(STEPS)]
            for m in range(STEPS):
                total = jnp.zeros((nb, nb), F32)
                for k in range(m, STEPS):
                    f = factor(k, m)
                    total += dot(jnp.concatenate([f[:nb], f[:nb], f[nb:2 * nb]], axis=1), solved[k])
                keep(b, m, total)

        if b == 0:
            for k in range(STEPS):
                @pl.when(gb == k)
                def _():
                    for m in range(STEPS):
                        if m <= k:
                            f = factor(k, m)
                            value = -(f[:nb].astype(F32) + f[nb:2 * nb].astype(F32))
                        else:
                            value = jnp.zeros((nb, nb), F32)
                        keep(b, m, value)

    def ready(g):
        a = g // n_prow
        i = jnp.where(a < first_level, (a + first_level * early - early) % max(first_level, 1), a)
        i = jnp.where(a < last, i, rb - 1 + last - swap(a))
        return i * SUB + SUB - 1

    first = jnp.maximum(ready(jnp.int32(1)), ready(jnp.int32(2)))
    when = [jnp.maximum(ready(block_of(2 + b)), first) for b in range(cb)]

    def tables(t):
        @pl.when(t == first)
        def _():
            for slot in range(2):
                wait_slot(slot)
                settle(slot)
            factors()

        for b in range(cb):
            @pl.when(t == when[b])
            def _():
                wait_slot(2 + b)
                settle(2 + b)
                columns(b, block_of(2 + b))

    def block(i, a, g, b):
        gb = block_of(2 + b)
        place_of = pl.ds(pl.multiple_of(a * nb, nb), nb)

        def product():
            return dot(prow_l[...], ccol[b])

        def updated():
            old = jnp.concatenate(
                [abuf[i % 2, pl.ds(b * 2 + h, nb, stride=stride), :] for h in range(2)], axis=1)
            return old - product()

        @pl.when((gb >= STEPS) & (g > gb))
        def _():
            panels[b, place_of, :] = updated()

        @pl.when((gb >= STEPS) & (g == gb))
        def _():
            down = lax.broadcasted_iota(jnp.int32, (nb, nb), 0)
            across = lax.broadcasted_iota(jnp.int32, (nb, nb), 1)
            panels[b, place_of, :] = jnp.where(down >= across, updated(), 0.0)

        if b == 0:
            @pl.when((gb < STEPS) & (g >= gb))
            def _():
                panels[b, place_of, :] = -product()

    def compute(u):
        i = lax.div(u, SUB)
        part = u - i * SUB
        a = place(i)
        g = a * n_prow + p

        @pl.when(part == 0)
        def _():
            @pl.when(i + 1 < done)
            def _():
                a_in(i + 1).start()

            @pl.when(g >= q)
            def _():
                for k in range(STEPS):
                    prow_l[:, k * 3 * nb:(k + 1) * 3 * nb] = left(
                        panels[k, pl.ds(pl.multiple_of(a * nb, nb), nb), :])
            a_in(i).wait()
            block(i, a, g, 0)

        for b in range(1, inner):
            pl.when(part == min(b, SUB - 1))(lambda: block(i, a, g, b))

    def step(t, carry):
        @pl.when(t < chunks)
        def _():
            s, w = spot(t), spot(t - WINDOW)

            @pl.when(z > 0)
            def _():
                z_in("wait_recv", s)
                pl.when(z < depth - 1)(lambda: start(z_out, s, w))
                start(x_out, s, w)
                start(c1_out, s, w)

            for k in range(STEPS):
                @pl.when(q == k)
                def _():
                    s_in(s).wait()
                    ahead = lax.rem(t, AHEAD)
                    for h in range(2):
                        panels[k, rows(s, 0, sub), h * 128:(h + 1) * 128] = sbuf[ahead, pl.ds(h, sub, stride=stride), :]
                    start(to_x(k), s, w)
                    start(to_sib(k), s, w)

                    @pl.when(t + AHEAD < chunks)
                    def _():
                        s_in(spot(t + AHEAD)).start()

        @pl.when((t >= HOP) & (t < chunks + HOP))
        def _():
            s, w = spot(t - HOP), spot(t - HOP - WINDOW)

            @pl.when(z > 0)
            def _():
                x_in("wait_recv", s)
                start(c2_out, s, w)

            pl.when(above)(lambda: start(dn_out, s, w))

            for k in range(STEPS):
                @pl.when(q == fwd_of(k))
                def _():
                    fwd(k)("wait_recv", s)
                    start(fwd(k), s, w)

        @pl.when((t >= FULL) & (t < chunks + FULL))
        def _():
            s = spot(t - FULL)

            @pl.when(z > 0)
            def _():
                c1_in("wait_recv", s)
                c2_in("wait_recv", s)

            @pl.when(z == 0)
            def _():
                for k in range(STEPS):
                    same = k + 1 - 2 * (k % 2)

                    @pl.when(q == same)
                    def _():
                        to_sib(k)("wait_recv", s)

                    @pl.when((q != k) & (q != same) & (q != fwd_of(k)))
                    def _():
                        fwd(k)("wait_recv", s)
                start(z_out, s, spot(t - FULL - WINDOW))

            pl.when(jnp.logical_not(low))(lambda: publish(s, s.kept))

        @pl.when(low & (t >= down) & (t < chunks + down + PAIR))
        def _():
            @pl.when(t < chunks + down)
            def _():
                s = spot(t - down)
                dn_in("wait_recv", s)
                start(dc_out, s, spot(t - down - WINDOW))

            @pl.when(t >= down + PAIR)
            def _():
                s = spot(t - down - PAIR)
                dc_in("wait_recv", s)
                publish(s, s.kept)

        tables(t - lag)

        v = t - lag + LAG - behind
        for extra in range(2):
            u = v + v // 4 + extra
            pl.when((v >= 0) & (u < done * SUB) & (v % 4 >= 3 * extra))(lambda: compute(u))
        return carry

    lag = jnp.where(low, down + PAIR, FULL) + LAG
    lax.fori_loop(0, jnp.maximum(chunks + lag, lag - LAG + behind + done * SUB), step, 0)

    pl.when(z < depth - 1)(lambda: drain(z_out))

    @pl.when(z > 0)
    def _():
        drain(x_out)
        drain(c1_out)
        drain(c2_out)

    pl.when(above)(lambda: drain(dn_out))
    pl.when(low)(lambda: drain(dc_out))

    for k in range(STEPS):
        @pl.when(q == k)
        def _():
            drain(to_x(k))
            drain(to_sib(k))

        @pl.when(q == fwd_of(k))
        def _():
            drain(fwd(k))


def update(n_prow, n_pcol, rb, cb, nb, done, a_hbm, panels, out_hbm, abuf, obuf, ccol, prow_l, asem, osem):
    p = lax.axis_index("prow")
    q = lax.axis_index("pcol")
    lines = nb * cb * 2
    stride = cb * 2
    heavy = rb - done
    full = cb - 1 if done == rb - min(n_pcol // n_prow, rb) else 0

    def span(a):
        return pl.ds(pl.multiple_of(a * lines, lines), lines)

    def a_in(j):
        return pltpu.make_async_copy(a_hbm.at[span(done + j), :], abuf.at[j % 2], asem.at[j % 2])

    def o_out(n, a):
        return pltpu.make_async_copy(obuf.at[n % DEEP], out_hbm.at[span(a), :], osem.at[n % DEEP])

    def put(n, b, value):
        for h in range(2):
            obuf[n % DEEP, pl.ds(b * 2 + h, nb, stride=stride), :] = value[:, h * 128:(h + 1) * 128]

    def old(j, b):
        return jnp.concatenate(
            [abuf[j % 2, pl.ds(b * 2 + h, nb, stride=stride), :] for h in range(2)], axis=1)

    def raw(k, a):
        return panels[k, pl.ds(pl.multiple_of(a * nb, nb), nb), :]

    def turn(n):
        @pl.when(n >= DEEP)
        def _():
            o_out(n - DEEP, 0).wait()

    def light(a, n):
        turn(n)
        g = a * n_prow + p
        for b in range(cb):
            gb = b * n_pcol + q
            if b < STEPS:
                pl.when(g >= gb)(lambda: put(n, b, raw(b, a)))
            pl.when((g < gb) | (b >= STEPS))(lambda: put(n, b, jnp.zeros((nb, nb), F32)))
        o_out(n, a).start()

    def dense(j, n, b, product):
        @pl.when(b * n_pcol + q >= STEPS)
        def _():
            put(n, b, old(j, b) - product)

        if b == 0:
            @pl.when(q < STEPS)
            def _():
                put(n, b, -product)

    def block(j, n, g, b):
        gb = b * n_pcol + q

        @pl.when(g > gb)
        def _():
            dense(j, n, b, dot(prow_l[...], ccol[:, b * nb:(b + 1) * nb]))

        @pl.when(g == gb)
        def _():
            product = dot(prow_l[...], ccol[:, b * nb:(b + 1) * nb])
            if b == 0:
                pl.when(q < STEPS)(lambda: put(n, b, -product))

            @pl.when(gb >= STEPS)
            def _():
                down = lax.broadcasted_iota(jnp.int32, (nb, nb), 0)
                across = lax.broadcasted_iota(jnp.int32, (nb, nb), 1)
                put(n, b, jnp.where(down >= across, old(j, b) - product, 0.0))

        @pl.when(g < gb)
        def _():
            put(n, b, jnp.zeros((nb, nb), F32))

    a_in(0).start()
    if heavy > 1:
        a_in(1).start()
    def step(j, carry):
        lo, hi = j * done // heavy, (j + 1) * done // heavy

        def one(a, inner):
            light(a, a + j)
            return inner

        lax.fori_loop(lo, hi, one, 0)

        @pl.when(j == 0)
        def _():
            for b in range(cb):
                for m in range(STEPS):
                    ccol[m * 3 * nb:(m + 1) * 3 * nb, b * nb:(b + 1) * nb] = right(
                        panels[m, (rb + b) * nb:(rb + b + 1) * nb, :])

        a, n = done + j, hi + j
        g = a * n_prow + p
        turn(n)
        for k in range(STEPS):
            prow_l[:, k * 3 * nb:(k + 1) * 3 * nb] = left(raw(k, a))
        a_in(j).wait()
        if full:
            product = dot(prow_l[...], ccol[:, :full * nb])
            for b in range(full):
                value = product[:, b * nb:(b + 1) * nb]
                put(n, b, (jnp.where(q < STEPS, 0.0, old(j, b)) if b == 0 else old(j, b)) - value)
        for b in range(full, cb):
            block(j, n, g, b)
        o_out(n, a).start()

        @pl.when(j + 2 < heavy)
        def _():
            a_in(j + 2).start()
        return carry

    lax.fori_loop(0, heavy, step, 0)
    for n in range(max(rb - DEEP, 0), rb):
        o_out(n, 0).wait()


def per_device(n_prow, n_pcol, matrix, inverses):
    rb, _, nb, cb, _, _ = matrix.shape
    lines = matrix.reshape(rb * nb * cb * 2, nb // 2)
    level = min(n_pcol // n_prow, rb)
    done = max(min(rb - max(level, WINDOW // SUB), STEPS * level), 0)
    vmem = pltpu.VMEM
    dma = pltpu.SemaphoreType.DMA
    anywhere = pl.BlockSpec(memory_space=pl.ANY)
    inside = pl.BlockSpec(memory_space=pltpu.VMEM)
    panels = pl.pallas_call(
        functools.partial(gather, n_prow, n_pcol, rb, cb, nb, done),
        out_shape=vmem((STEPS, (rb + cb) * nb, nb), F32),
        in_specs=[anywhere, inside],
        out_specs=inside,
        scratch_shapes=[
            vmem((2 + cb, STEPS, nb, nb), F32),
            vmem((AHEAD, nb // SUB * cb * 2, 128), F32),
            vmem((2, nb * cb * 2, 128), F32),
            vmem((STEPS, 3 * STEPS * nb, nb), BF),
            vmem((min(cb, STEPS), 3 * STEPS * nb, nb), BF),
            vmem((nb, 3 * STEPS * nb), BF),
            dma((rb * SUB, 5)),
            dma((WINDOW, 8)),
            dma((2 + cb, SUB)),
            dma((2 + cb, SUB, n_prow)),
            dma((AHEAD,)),
            dma((2,)),
        ],
        compiler_params=pltpu.CompilerParams(
            collective_id=0, has_side_effects=True, vmem_limit_bytes=24 * 1024 * 1024
        ),
    )(lines, inverses)
    out = pl.pallas_call(
        functools.partial(update, n_prow, n_pcol, rb, cb, nb, done),
        out_shape=jax.ShapeDtypeStruct(lines.shape, F32),
        in_specs=[anywhere, inside],
        out_specs=anywhere,
        scratch_shapes=[
            vmem((2, nb * cb * 2, 128), F32),
            vmem((DEEP, nb * cb * 2, 128), F32),
            vmem((3 * STEPS * nb, cb * nb), BF),
            vmem((nb, 3 * STEPS * nb), BF),
            dma((2,)),
            dma((DEEP,)),
        ],
        compiler_params=pltpu.CompilerParams(vmem_limit_bytes=24 * 1024 * 1024),
    )(lines, panels)
    return out.reshape(matrix.shape)


def solution(mesh):
    in_specs = (P(None, "prow", None, None, "pcol", None), P())
    out_specs = P(None, "prow", None, None, "pcol", None)
    return jax.shard_map(
        functools.partial(per_device, mesh.shape["prow"], mesh.shape["pcol"]),
        mesh=mesh, in_specs=in_specs, out_specs=out_specs, check_vma=False,
    )
```

```python
import functools
import types

import jax
import jax.numpy as jnp
from jax import lax
from jax.experimental import pallas as pl
from jax.experimental.pallas import tpu as pltpu
from jax.sharding import PartitionSpec as P

STEPS = 3
SUB = 2
WINDOW = 8
LAG = 5
AHEAD = 4
HOP = 3
FULL = 4
PAIR = 1
BACK = 11
DEEP = 6
MESH = pl.DeviceIdType.MESH
BF = jnp.bfloat16
F32 = jnp.float32


def split(value):
    high = value.astype(BF)
    return high, (value - high.astype(F32)).astype(BF)


def left(value):
    high, low = split(value)
    return jnp.concatenate([high, high, low], axis=1)


def right(value):
    high, low = split(value)
    return jnp.concatenate([high, low, high], axis=0)


def dot(a, b):
    return lax.dot_general(a, b, (((1,), (0,)), ((), ())), preferred_element_type=F32)


def gather(
    n_prow, n_pcol, rb, cb, nb, done,
    a_hbm, inv_ref, panels,
    xch, sbuf, abuf, cst, ccol, prow_l,
    rsem, ssem, xrsem, xssem, srcsem, asem,
):
    p = lax.axis_index("prow")
    q = lax.axis_index("pcol")
    depth = n_pcol // 4
    z, x, c = q // 4, (q // 2) % 2, q % 2
    sib = q + 1 - 2 * c
    xn = q + 2 - 4 * x
    sub = nb // SUB
    quarter = sub // 4
    chunks = rb * SUB
    lines = nb * cb * 2
    sub_lines = sub * cb * 2
    stride = cb * 2
    slots = 2 + cb
    inner = ccol.shape[0]
    level = min(n_pcol // n_prow, rb)
    last = rb - level
    first_level = min(level, last)
    early = 3 // n_prow + 1
    behind = LAG + SUB * level
    down = FULL + BACK

    barrier = pltpu.get_barrier_semaphore()

    def greet(pp, qq):
        pl.semaphore_signal(barrier, inc=1, device_id=(pp, qq), device_id_type=MESH)

    greet(p, sib)
    greet(p, xn)
    pl.when(z > 0)(lambda: greet(p, q - 4))
    pl.when(z < depth - 1)(lambda: greet(p, q + 4))
    for d in range(1, n_prow):
        greet((p + d) % n_prow, q)
    peers = 1 + n_prow + (z > 0).astype(jnp.int32) + (z < depth - 1).astype(jnp.int32)

    def swap(a):
        if level < 3:
            return a
        return jnp.where(a == last + 1, last + 2, jnp.where(a == last + 2, last + 1, a))

    def place(i):
        turned = i + early % max(first_level, 1)
        a = jnp.where(i < first_level, jnp.where(turned >= first_level, turned - first_level, turned), i)
        return jnp.where(i < last, a, swap(rb - 1 + last - i))

    def spot(n):
        i = lax.div(n, SUB)
        part = n - i * SUB
        a = place(i)
        g = a * n_prow + p
        live = n >= 0
        seed = (g == 1) | (g == 2)
        here = live & (seed | (g >= 4 * z))
        beyond = live & (seed | (g >= 4 * (z + 1)))
        near = g < 4
        return types.SimpleNamespace(
            n=n, part=part, a=a, line=a * SUB + part, row=(a * SUB + part) * sub, slot=lax.rem(n, WINDOW),
            live=(live & near, live & jnp.logical_not(near)), here=(here & near, here & jnp.logical_not(near)),
            beyond=(beyond & near, beyond & jnp.logical_not(near)), kept=here, always=live)

    def rows(s, first, count):
        return pl.ds(pl.multiple_of(s.row + first, quarter), count)

    def remote(ref, s, dev, si, ri):
        return pltpu.make_async_remote_copy(
            src_ref=ref, dst_ref=ref, send_sem=ssem.at[s.slot, si], recv_sem=rsem.at[s.n, ri],
            device_id=(p, dev), device_id_type=MESH,
        )

    def cp_q(s, count, j, dev, si, ri):
        return remote(panels.at[pl.ds(0, count), rows(s, j * quarter, quarter), :], s, dev, si, ri)

    def cp_k(s, k, dev, si):
        return remote(panels.at[k, rows(s, 0, sub), :], s, dev, si, k)

    def cp_half(s, k, dev, si):
        return remote(panels.at[k, rows(s, sub // 2, sub // 2), :], s, dev, si, k)

    def either(yes, no, needed):
        def act(method, s):
            near, far = getattr(s, needed)
            pl.when(near)(lambda: getattr(yes(s), method)())
            pl.when(far)(lambda: getattr(no(s), method)())
        return act

    def start(act, s, w):
        act("wait_send", w)
        act("start", s)

    def drain(act):
        for n in range(max(chunks - WINDOW, 0), chunks):
            act("wait_send", spot(jnp.int32(n)))

    mine = 2 * x + c
    other = 2 * (1 - x) + c
    up = jnp.minimum(q + 4, n_pcol - 1)

    def quarters(j, dev, si, needed):
        return either(lambda s: cp_q(s, 2, j, dev, si, si), lambda s: cp_q(s, STEPS, j, dev, si, si), needed)

    z_out = quarters(mine, up, 0, "beyond")
    x_out = quarters(mine, xn, 1, "here")
    c1_out = quarters(mine, sib, 2, "here")
    c2_out = quarters(other, sib, 3, "here")
    z_in = quarters(mine, sib, 0, "here")
    x_in = quarters(other, sib, 1, "here")
    c1_in = quarters(2 * x + 1 - c, sib, 2, "here")
    c2_in = quarters(2 * (1 - x) + 1 - c, sib, 3, "here")

    low = (z == 0) & (x == 1)
    above = (z == 1) & (x == 1)

    def two(j, dev, si, ri):
        return lambda method, s: pl.when(s.live[1])(lambda: getattr(cp_q(s, 2, j, dev, si, ri), method)())

    dn_out = two(c, jnp.maximum(q - 4, 0), 4, 3)
    dn_in = two(c, sib, 4, 3)
    dc_out = two(c, sib, 7, 4)
    dc_in = two(1 - c, sib, 7, 4)

    def whole(k, dev, si):
        return lambda method, s: pl.when(s.always)(lambda: getattr(cp_k(s, k, dev, si), method)())

    def hop(k, dev):
        if k < 2:
            return either(
                lambda s: cp_k(s, k, dev, 1 + 2 * k), lambda s: cp_half(s, k, dev, 1 + 2 * k), "live")
        return whole(k, dev, 1 + 2 * k)

    def to_x(k):
        return hop(k, xn)

    def to_sib(k):
        return whole(k, sib, 2 + 2 * k)

    def fwd(k):
        return hop(k, sib)

    def fwd_of(k):
        return k + 2 - 4 * ((k // 2) % 2)

    def block_of(slot):
        return slot + 1 if slot < 2 else (slot - 2) * n_pcol + q

    def depth_of(slot):
        return min(slot + 1, STEPS)

    def used(slot):
        return block_of(slot) >= (0 if slot < 2 else STEPS)

    def cp_x(slot, s, part, d):
        return pltpu.make_async_remote_copy(
            src_ref=panels.at[pl.ds(0, depth_of(slot)), rows(s, 0, sub), :],
            dst_ref=xch.at[slot, pl.ds(0, depth_of(slot)), pl.ds(part * sub, sub), :],
            send_sem=xssem.at[slot, part, d], recv_sem=xrsem.at[slot, part],
            device_id=((p + d) % n_prow, q), device_id_type=MESH,
        )

    def cp_l(slot, s, part):
        return pltpu.make_async_copy(
            panels.at[pl.ds(0, depth_of(slot)), rows(s, 0, sub), :],
            xch.at[slot, pl.ds(0, depth_of(slot)), pl.ds(part * sub, sub), :], xrsem.at[slot, part])

    owned = [used(slot) & (block_of(slot) % n_prow == p) for slot in range(slots)]
    taken = [used(slot) & (block_of(slot) % n_prow != p) for slot in range(slots)]
    owner = [block_of(slot) // n_prow for slot in range(slots)]
    zero = spot(jnp.int32(0))

    def publish(s, wanted):
        for slot in range(slots):
            @pl.when(wanted & owned[slot] & (owner[slot] == s.a))
            def _():
                for d in range(1, n_prow):
                    cp_x(slot, s, s.part, d).start()
                cp_l(slot, s, s.part).start()

    def wait_slot(slot):
        @pl.when(owned[slot])
        def _():
            for part in range(SUB):
                cp_l(slot, zero, part).wait()

        @pl.when(taken[slot])
        def _():
            for part in range(SUB):
                cp_x(slot, zero, part, 1).wait_recv()

    def settle(slot):
        @pl.when(owned[slot])
        def _():
            for part in range(SUB):
                for d in range(1, n_prow):
                    cp_x(slot, zero, part, d).wait_send()

    def a_in(i):
        return pltpu.make_async_copy(
            a_hbm.at[pl.ds(pl.multiple_of(place(i) * lines, lines), lines), :], abuf.at[i % 2], asem.at[i % 2])

    def s_in(s):
        ahead = lax.rem(s.n, AHEAD)
        return pltpu.make_async_copy(
            a_hbm.at[pl.ds(pl.multiple_of(s.line * sub_lines, sub_lines), sub_lines), :],
            sbuf.at[ahead], srcsem.at[ahead])

    @pl.when(q < STEPS)
    def _():
        for n in range(min(AHEAD, chunks)):
            s_in(spot(jnp.int32(n))).start()

    if done > 0:
        a_in(jnp.int32(0)).start()
    pl.semaphore_wait(barrier, peers)

    def factor(k, m):
        return cst[k, m * 3 * nb:(m + 1) * 3 * nb, :]

    def factors():
        def mul(u, v):
            return dot(left(u), right(v))

        r00, r11, r22 = inv_ref[0].T, inv_ref[1].T, inv_ref[2].T
        w10 = mul(xch[0, 0], r00)
        w20 = mul(xch[1, 0], r00)
        r01 = -mul(mul(r00, w10.T), r11)
        w21 = mul(xch[1, 0], r01) + mul(xch[1, 1], r11)
        r02 = -mul(mul(r00, w20.T) + mul(r01, w21.T), r22)
        r12 = -mul(mul(r11, w21.T), r22)
        for k, column in enumerate(((r00,), (r01, r11), (r02, r12, r22))):
            for m, value in enumerate(column):
                cst[k, m * 3 * nb:(m + 1) * 3 * nb, :] = right(value)

    def keep(b, m, value):
        panels[m, (rb + b) * nb:(rb + b + 1) * nb, :] = value
        if b < inner:
            ccol[b, m * 3 * nb:(m + 1) * 3 * nb, :] = right(value)

    def columns(b, gb):
        @pl.when(gb >= STEPS)
        def _():
            raw = jnp.concatenate([left(xch[2 + b, m]) for m in range(STEPS)], axis=1)
            solved = [
                right(dot(raw[:, :(k + 1) * 3 * nb], cst[k, :(k + 1) * 3 * nb, :]).T) for k in range(STEPS)]
            for m in range(STEPS):
                total = jnp.zeros((nb, nb), F32)
                for k in range(m, STEPS):
                    f = factor(k, m)
                    total += dot(jnp.concatenate([f[:nb], f[:nb], f[nb:2 * nb]], axis=1), solved[k])
                keep(b, m, total)

        if b == 0:
            for k in range(STEPS):
                @pl.when(gb == k)
                def _():
                    for m in range(STEPS):
                        if m <= k:
                            f = factor(k, m)
                            value = -(f[:nb].astype(F32) + f[nb:2 * nb].astype(F32))
                        else:
                            value = jnp.zeros((nb, nb), F32)
                        keep(b, m, value)

    def ready(g):
        a = g // n_prow
        i = jnp.where(a < first_level, (a + first_level * early - early) % max(first_level, 1), a)
        i = jnp.where(a < last, i, rb - 1 + last - swap(a))
        return i * SUB + SUB - 1

    first = jnp.maximum(ready(jnp.int32(1)), ready(jnp.int32(2)))
    when = [jnp.maximum(ready(block_of(2 + b)), first) for b in range(cb)]

    def tables(t):
        @pl.when(t == first)
        def _():
            for slot in range(2):
                wait_slot(slot)
                settle(slot)
            factors()

        for b in range(cb):
            @pl.when(t == when[b])
            def _():
                wait_slot(2 + b)
                settle(2 + b)
                columns(b, block_of(2 + b))

    def block(i, a, g, b):
        gb = block_of(2 + b)
        place_of = pl.ds(pl.multiple_of(a * nb, nb), nb)

        def product():
            return dot(prow_l[...], ccol[b])

        def updated():
            old = jnp.concatenate(
                [abuf[i % 2, pl.ds(b * 2 + h, nb, stride=stride), :] for h in range(2)], axis=1)
            return old - product()

        @pl.when((gb >= STEPS) & (g > gb))
        def _():
            panels[b, place_of, :] = updated()

        @pl.when((gb >= STEPS) & (g == gb))
        def _():
            down = lax.broadcasted_iota(jnp.int32, (nb, nb), 0)
            across = lax.broadcasted_iota(jnp.int32, (nb, nb), 1)
            panels[b, place_of, :] = jnp.where(down >= across, updated(), 0.0)

        if b == 0:
            @pl.when((gb < STEPS) & (g >= gb))
            def _():
                panels[b, place_of, :] = -product()

    def compute(u):
        i = lax.div(u, SUB)
        part = u - i * SUB
        a = place(i)
        g = a * n_prow + p

        @pl.when(part == 0)
        def _():
            @pl.when(i + 1 < done)
            def _():
                a_in(i + 1).start()

            @pl.when(g >= q)
            def _():
                for k in range(STEPS):
                    prow_l[:, k * 3 * nb:(k + 1) * 3 * nb] = left(
                        panels[k, pl.ds(pl.multiple_of(a * nb, nb), nb), :])
            a_in(i).wait()
            block(i, a, g, 0)

        for b in range(1, inner):
            pl.when(part == min(b, SUB - 1))(lambda: block(i, a, g, b))

    def step(t, carry):
        @pl.when(t < chunks)
        def _():
            s, w = spot(t), spot(t - WINDOW)

            @pl.when(z > 0)
            def _():
                z_in("wait_recv", s)
                pl.when(z < depth - 1)(lambda: start(z_out, s, w))
                start(x_out, s, w)
                start(c1_out, s, w)

            for k in range(STEPS):
                @pl.when(q == k)
                def _():
                    s_in(s).wait()
                    ahead = lax.rem(t, AHEAD)
                    for h in range(2):
                        panels[k, rows(s, 0, sub), h * 128:(h + 1) * 128] = sbuf[ahead, pl.ds(h, sub, stride=stride), :]
                    start(to_x(k), s, w)
                    start(to_sib(k), s, w)

                    @pl.when(t + AHEAD < chunks)
                    def _():
                        s_in(spot(t + AHEAD)).start()

        @pl.when((t >= HOP) & (t < chunks + HOP))
        def _():
            s, w = spot(t - HOP), spot(t - HOP - WINDOW)

            @pl.when(z > 0)
            def _():
                x_in("wait_recv", s)
                start(c2_out, s, w)

            pl.when(above)(lambda: start(dn_out, s, w))

            for k in range(STEPS):
                @pl.when(q == fwd_of(k))
                def _():
                    fwd(k)("wait_recv", s)
                    start(fwd(k), s, w)

        @pl.when((t >= FULL) & (t < chunks + FULL))
        def _():
            s = spot(t - FULL)

            @pl.when(z > 0)
            def _():
                c1_in("wait_recv", s)
                c2_in("wait_recv", s)

            @pl.when(z == 0)
            def _():
                for k in range(STEPS):
                    same = k + 1 - 2 * (k % 2)

                    @pl.when(q == same)
                    def _():
                        to_sib(k)("wait_recv", s)

                    @pl.when((q != k) & (q != same) & (q != fwd_of(k)))
                    def _():
                        fwd(k)("wait_recv", s)
                start(z_out, s, spot(t - FULL - WINDOW))

            pl.when(jnp.logical_not(low))(lambda: publish(s, s.kept))

        @pl.when(low & (t >= down) & (t < chunks + down + PAIR))
        def _():
            @pl.when(t < chunks + down)
            def _():
                s = spot(t - down)
                dn_in("wait_recv", s)
                start(dc_out, s, spot(t - down - WINDOW))

            @pl.when(t >= down + PAIR)
            def _():
                s = spot(t - down - PAIR)
                dc_in("wait_recv", s)
                publish(s, s.kept)

        tables(t - lag)

        v = t - lag + LAG - behind
        for extra in range(2):
            u = v + v // 4 + extra
            pl.when((v >= 0) & (u < done * SUB) & (v % 4 >= 3 * extra))(lambda: compute(u))
        return carry

    lag = jnp.where(low, down + PAIR, FULL) + LAG
    lax.fori_loop(0, jnp.maximum(chunks + lag, lag - LAG + behind + done * SUB), step, 0)

    pl.when(z < depth - 1)(lambda: drain(z_out))

    @pl.when(z > 0)
    def _():
        drain(x_out)
        drain(c1_out)
        drain(c2_out)

    pl.when(above)(lambda: drain(dn_out))
    pl.when(low)(lambda: drain(dc_out))

    for k in range(STEPS):
        @pl.when(q == k)
        def _():
            drain(to_x(k))
            drain(to_sib(k))

        @pl.when(q == fwd_of(k))
        def _():
            drain(fwd(k))


def update(n_prow, n_pcol, rb, cb, nb, done, a_hbm, panels, out_hbm, abuf, obuf, ccol, prow_l, asem, osem):
    p = lax.axis_index("prow")
    q = lax.axis_index("pcol")
    lines = nb * cb * 2
    stride = cb * 2
    heavy = rb - done
    full = cb - 1 if done == rb - min(n_pcol // n_prow, rb) else 0

    def span(a):
        return pl.ds(pl.multiple_of(a * lines, lines), lines)

    def a_in(j):
        return pltpu.make_async_copy(a_hbm.at[span(done + j), :], abuf.at[j % 2], asem.at[j % 2])

    def o_out(n, a):
        return pltpu.make_async_copy(obuf.at[n % DEEP], out_hbm.at[span(a), :], osem.at[n % DEEP])

    def put(n, b, value):
        for h in range(2):
            obuf[n % DEEP, pl.ds(b * 2 + h, nb, stride=stride), :] = value[:, h * 128:(h + 1) * 128]

    def old(j, b):
        return jnp.concatenate(
            [abuf[j % 2, pl.ds(b * 2 + h, nb, stride=stride), :] for h in range(2)], axis=1)

    def raw(k, a):
        return panels[k, pl.ds(pl.multiple_of(a * nb, nb), nb), :]

    def turn(n):
        @pl.when(n >= DEEP)
        def _():
            o_out(n - DEEP, 0).wait()

    def light(a, n):
        turn(n)
        g = a * n_prow + p
        for b in range(cb):
            gb = b * n_pcol + q
            if b < STEPS:
                pl.when(g >= gb)(lambda: put(n, b, raw(b, a)))
            pl.when((g < gb) | (b >= STEPS))(lambda: put(n, b, jnp.zeros((nb, nb), F32)))
        o_out(n, a).start()

    def dense(j, n, b, product):
        @pl.when(b * n_pcol + q >= STEPS)
        def _():
            put(n, b, old(j, b) - product)

        if b == 0:
            @pl.when(q < STEPS)
            def _():
                put(n, b, -product)

    def block(j, n, g, b):
        gb = b * n_pcol + q

        @pl.when(g > gb)
        def _():
            dense(j, n, b, dot(prow_l[...], ccol[:, b * nb:(b + 1) * nb]))

        @pl.when(g == gb)
        def _():
            product = dot(prow_l[...], ccol[:, b * nb:(b + 1) * nb])
            if b == 0:
                pl.when(q < STEPS)(lambda: put(n, b, -product))

            @pl.when(gb >= STEPS)
            def _():
                down = lax.broadcasted_iota(jnp.int32, (nb, nb), 0)
                across = lax.broadcasted_iota(jnp.int32, (nb, nb), 1)
                put(n, b, jnp.where(down >= across, old(j, b) - product, 0.0))

        @pl.when(g < gb)
        def _():
            put(n, b, jnp.zeros((nb, nb), F32))

    a_in(0).start()
    if heavy > 1:
        a_in(1).start()
    def step(j, carry):
        lo, hi = j * done // heavy, (j + 1) * done // heavy

        def one(a, inner):
            light(a, a + j)
            return inner

        lax.fori_loop(lo, hi, one, 0)

        @pl.when(j == 0)
        def _():
            for b in range(cb):
                for m in range(STEPS):
                    ccol[m * 3 * nb:(m + 1) * 3 * nb, b * nb:(b + 1) * nb] = right(
                        panels[m, (rb + b) * nb:(rb + b + 1) * nb, :])

        a, n = done + j, hi + j
        g = a * n_prow + p
        turn(n)
        for k in range(STEPS):
            prow_l[:, k * 3 * nb:(k + 1) * 3 * nb] = left(raw(k, a))
        a_in(j).wait()
        if full:
            product = dot(prow_l[...], ccol[:, :full * nb])
            for b in range(full):
                value = product[:, b * nb:(b + 1) * nb]
                put(n, b, (jnp.where(q < STEPS, 0.0, old(j, b)) if b == 0 else old(j, b)) - value)
        for b in range(full, cb):
            block(j, n, g, b)
        o_out(n, a).start()

        @pl.when(j + 2 < heavy)
        def _():
            a_in(j + 2).start()
        return carry

    lax.fori_loop(0, heavy, step, 0)
    for n in range(max(rb - DEEP, 0), rb):
        o_out(n, 0).wait()


def per_device(n_prow, n_pcol, matrix, inverses):
    rb, _, nb, cb, _, _ = matrix.shape
    lines = matrix.reshape(rb * nb * cb * 2, nb // 2)
    level = min(n_pcol // n_prow, rb)
    done = max(min(rb - max(level, WINDOW // SUB), STEPS * level), 0)
    vmem = pltpu.VMEM
    dma = pltpu.SemaphoreType.DMA
    anywhere = pl.BlockSpec(memory_space=pl.ANY)
    inside = pl.BlockSpec(memory_space=pltpu.VMEM)
    panels = pl.pallas_call(
        functools.partial(gather, n_prow, n_pcol, rb, cb, nb, done),
        out_shape=vmem((STEPS, (rb + cb) * nb, nb), F32),
        in_specs=[anywhere, inside],
        out_specs=inside,
        scratch_shapes=[
            vmem((2 + cb, STEPS, nb, nb), F32),
            vmem((AHEAD, nb // SUB * cb * 2, 128), F32),
            vmem((2, nb * cb * 2, 128), F32),
            vmem((STEPS, 3 * STEPS * nb, nb), BF),
            vmem((min(cb, STEPS), 3 * STEPS * nb, nb), BF),
            vmem((nb, 3 * STEPS * nb), BF),
            dma((rb * SUB, 5)),
            dma((WINDOW, 8)),
            dma((2 + cb, SUB)),
            dma((2 + cb, SUB, n_prow)),
            dma((AHEAD,)),
            dma((2,)),
        ],
        compiler_params=pltpu.CompilerParams(
            collective_id=0, has_side_effects=True, vmem_limit_bytes=24 * 1024 * 1024
        ),
    )(lines, inverses)
    out = pl.pallas_call(
        functools.partial(update, n_prow, n_pcol, rb, cb, nb, done),
        out_shape=jax.ShapeDtypeStruct(lines.shape, F32),
        in_specs=[anywhere, inside],
        out_specs=anywhere,
        scratch_shapes=[
            vmem((2, nb * cb * 2, 128), F32),
            vmem((DEEP, nb * cb * 2, 128), F32),
            vmem((3 * STEPS * nb, cb * nb), BF),
            vmem((nb, 3 * STEPS * nb), BF),
            dma((2,)),
            dma((DEEP,)),
        ],
        compiler_params=pltpu.CompilerParams(vmem_limit_bytes=24 * 1024 * 1024),
    )(lines, panels)
    return out.reshape(matrix.shape)


def solution(mesh):
    in_specs = (P(None, "prow", None, None, "pcol", None), P())
    out_specs = P(None, "prow", None, None, "pcol", None)
    return jax.shard_map(
        functools.partial(per_device, mesh.shape["prow"], mesh.shape["pcol"]),
        mesh=mesh, in_specs=in_specs, out_specs=out_specs, check_vma=False,
    )
```
